512 devices in a mesh: obs: 8 (over x, core), dt: 64 (over y, z).
Axes of the slice: x: 4, y: 4, z: 16, core: 2. Of those that a mesh axis runs over, the one named last changes fastest.
Arguments:
- sky_map: float32 [512, 3, 512], P(('obs', 'dt')), may hold values from -6 to 6
- submap_of: int32 [8, 128, 16384], P('obs', None, 'dt'), may hold values from 0 to 511, as said below
- pixel_cell: int32 [8, 128, 16384], P('obs', None, 'dt'), may hold values from 0 to 511
- angles: float32 [8, 128, 16384], P('obs', None, 'dt'), may hold values from -3.140625 to 3.140625
- intervals: int32 [8, 16384], P('obs', 'dt'), may hold values from 0 to 31, never falling along the last dimension, each value on 1 to 1024 neighbouring positions
- wafer_of: int32 [8, 128], P('obs'), may hold values from 0 to 3
- mixing: bfloat16 [8, 128, 128], P('obs'), may hold values from -1 to 1
- knee: float32 [8, 128], P('obs'), may hold values from 2 to 200
Outputs:
- sky_out: float32 [512, 3, 512], P(('obs', 'dt'))
The draws below stay inside these ranges and needn't reach their ends.
Inputs may be any that keep to these rules, and one draw needn't show every extreme that they name: `submap_of`: the submaps of observation o lie in o * 64 to (o + 2) * 64 - 1, counted modulo 512.
All inputs are finite; a program needn't handle non-finite values.
Results may differ from the reference program's by a relative error of at most 0.00097.
Values sent between devices are 32-bit elements; how exact they have to be, the bound alone decides.
A program may use at most 128 MiB of HBM per device.

```python
import math
import jax
import jax.numpy as jnp
import numpy as np
from jax import lax

NSAMP = 16384
DET = 128
PIXSUB = 512
WAFERS = 4
SEGS = 32
OBS = 8
NSUB = 512
NPIX = 262144
N_DT = 64


def draw_submap_of(key, part):
    offsets = jax.random.randint(key, (OBS, DET, NSAMP), 0, 2 * N_DT)
    starts = jnp.arange(OBS) * N_DT
    result = (starts[:, None, None] + offsets) % NSUB
    result = result.at[OBS - 1, 0, 0].set(NSUB - 1)
    result = result.at[OBS - 1, 0, 1].set(0)
    return result.astype(jnp.int32)


def plant(entries, stream_key, least, high):
    extent = entries.shape
    index_at = [jax.random.randint(jax.random.fold_in(stream_key, axis), (), 0, extent[axis]) for axis in range(len(extent))]
    entries = entries.at[tuple(index_at)].set(least)
    longest = extent.index(max(extent))
    index_at[longest] = (index_at[longest] + 1) % extent[longest]
    return entries.at[tuple(index_at)].set(high)


def level_of(key, dims, cuts, smallest, top_value):
    loudness, own = 1.0, jax.random.fold_in(key, 6)
    for dim, parts in cuts:
        heights = jnp.exp(jax.random.uniform(jax.random.fold_in(own, dim), (parts,), jnp.float32, smallest / len(cuts), top_value / len(cuts)))
        loudness = loudness * jnp.repeat(heights, dims[dim] // parts).reshape([-1 if axis == dim else 1 for axis in range(len(dims))])
    return loudness


def length_profile(amount, total, reach, slope):
    weights = [(1 << 20) // math.isqrt(grade ** slope) + 1 for grade in range(2, amount + 1)]
    surplus, counts = total - reach - (amount - 1), [1] * (amount - 1)
    while surplus > 0:
        movable = [i for i in range(amount - 1) if counts[i] < reach]
        pool, remaining = sum([weights[i] for i in movable]), surplus
        for i in movable:
            addition = min(reach - counts[i], max(1, remaining * weights[i] // pool), surplus)
            counts[i] = counts[i] + addition
            surplus = surplus - addition
    return np.array([reach] + counts)


def ragged_sizes(key, number_of, total, limit, slope):
    if number_of == 2:
        one = jax.random.randint(key, (), max(1, total - limit), min(limit, total - 1) + 1)
        return jnp.stack([one, total - one])
    tallies = jnp.asarray(length_profile(number_of, total, limit, slope), jnp.int32)
    couples = (number_of - 1) // 2
    giver, receiver = tallies[1:1 + 2 * couples:2], tallies[2:2 + 2 * couples:2]
    slack = jnp.minimum(giver - 1, limit - receiver)
    passed = jax.random.randint(jax.random.fold_in(key, 1), (couples,), 0, 1 << 20) % (slack + 1)
    tallies = tallies.at[1:1 + 2 * couples:2].set(giver - passed).at[2:2 + 2 * couples:2].set(receiver + passed)
    return tallies[jax.random.permutation(jax.random.fold_in(key, 2), number_of)]


def centred(rng, shape, spread, reach, split=(), held_as=jnp.bfloat16):
    gain = level_of(rng, shape, split, -0.22, 0.18) if split else 1.0
    entries = jax.random.normal(rng, shape, jnp.float32) * spread * gain
    return jnp.minimum(jnp.maximum(entries, -reach), reach).astype(held_as)


def setup_inputs(seed: int = 0) -> dict:
    streams_of = jax.random.split(jax.random.key(seed), 9)
    return {
        "sky_map": centred(streams_of[0], (NSUB, 3, PIXSUB), 1.0, 6.0, ((0, 512),), jnp.float32),
        "submap_of": draw_submap_of(jax.random.fold_in(streams_of[8], 71), 0),
        "pixel_cell": plant(jax.random.randint(streams_of[2], (OBS, DET, NSAMP), 0, PIXSUB), jax.random.fold_in(streams_of[2], 1), 0, PIXSUB - 1).astype(jnp.int32),
        "angles": jnp.clip(jax.random.uniform(streams_of[3], (OBS, DET, NSAMP), jnp.float32, -3.140625, 3.140625), -3.140625, 3.140625),
        "intervals": jax.vmap(lambda own: jnp.searchsorted(jnp.cumsum(ragged_sizes(own, SEGS, NSAMP, NSAMP // 16, 2)), jnp.arange(NSAMP), side="right"))(jax.random.split(streams_of[4], OBS)).reshape((OBS, NSAMP)).astype(jnp.int32),
        "wafer_of": plant(jax.random.randint(streams_of[5], (OBS, DET), 0, WAFERS), jax.random.fold_in(streams_of[5], 1), 0, WAFERS - 1).astype(jnp.int32),
        "mixing": centred(streams_of[6], (OBS, DET, DET), (DET // WAFERS) ** -0.5, 1.0, ((0, 8),)),
        "knee": jnp.clip(jnp.exp(math.log(200.0) - 4.6051702 * jax.random.uniform(streams_of[7], (OBS, DET), jnp.float32) ** level_of(streams_of[7], (OBS, DET), ((0, 8),), -0.2, 0.2)), 2.0, 200.0),
    }


def reference(sky_map, submap_of, pixel_cell, angles, intervals, wafer_of, mixing, knee):
    flat_map = jnp.transpose(sky_map, (1, 0, 2)).reshape(3, -1)
    freqs = jnp.arange(NSAMP // 2 + 1).astype(jnp.float32)

    def one_obs(total, inputs):
        sub, cell, ang, seg, waf, mix, kn = inputs
        pix = (sub * PIXSUB + cell).astype(jnp.int32)
        keep_mask = (seg % 2 == 0).astype(jnp.float32)
        sampled = flat_map[:, pix]
        cos_weight = jnp.cos(2.0 * ang)
        sin_weight = jnp.sin(2.0 * ang)
        tod = keep_mask[None, :] * (sampled[0] + cos_weight * sampled[1] + sin_weight * sampled[2])
        same = waf[:, None] == waf[None, :]
        masked = jnp.where(same, mix, jnp.zeros_like(mix))
        corr = tod + jnp.dot(masked, tod.astype(jnp.bfloat16), preferred_element_type=jnp.float32)
        spectrum = jnp.fft.rfft(corr, axis=-1)
        weight = freqs[None, :] ** 2 / (freqs[None, :] ** 2 + kn[:, None] ** 2)
        filt = jnp.fft.irfft(spectrum * weight, n=NSAMP, axis=-1)
        weighted = keep_mask[None, :] * filt
        contrib = jnp.stack([weighted, weighted * cos_weight, weighted * sin_weight]).reshape(3, -1)
        total = total.at[:, pix.reshape(-1)].add(contrib)
        return total, None

    start = jnp.zeros((3, NPIX), jnp.float32)
    total, _ = lax.scan(one_obs, start, (submap_of, pixel_cell, angles, intervals, wafer_of, mixing, knee))
    return jnp.transpose(total.reshape(3, NSUB, PIXSUB), (1, 0, 2))
```

```python
import math

import jax
import jax.numpy as jnp
import ml_dtypes
import numpy as np
from jax import lax
from jax.experimental import pallas as pl
from jax.experimental.pallas import tpu as pltpu
from jax.sharding import PartitionSpec as P

MESH = pl.DeviceIdType.MESH
f32, bf16, i32 = jnp.float32, jnp.bfloat16, jnp.int32

DET = 128
SPAN = 256
PIX = 512
GROUP = 64
NY, NZ = 4, 16
WINDOW = 2 * GROUP
NSAMP = GROUP * SPAN
TILE = 8


def split_np(x):
    high = x.astype(ml_dtypes.bfloat16)
    low = (x - high.astype(np.float64)).astype(ml_dtypes.bfloat16)
    return high, low


def dft_tables():
    n = 128
    row = np.arange(256)
    row_det, row_n1 = (row // 2) % 2, 2 * (row // 4) + row % 2
    col_det, col_k1 = row // n, row % n
    same = (row_det[:, None] == col_det[None, :]).astype(np.float64)
    turn = 2.0 * np.pi * ((row_n1[:, None] * col_k1[None, :]) % n) / n
    cos_part, sin_part = same * np.cos(turn), -same * np.sin(turn)
    last = np.concatenate([cos_part, sin_part], axis=1)
    first = np.ascontiguousarray(last.T)
    index = np.arange(n)
    angle = 2.0 * np.pi * ((index[:, None] * index[None, :]) % n) / n
    c, s = np.cos(angle), np.sin(angle)
    forward = np.block([[c, -s], [s, c]])
    backward = np.block([[c, s], [-s, c]]) / NSAMP
    twist = 2.0 * np.pi * (col_k1[:, None] * index[None, :]) / NSAMP
    tables = []
    for x in (first, forward, backward, last):
        tables.extend(split_np(x))
    tables.extend([np.cos(twist).astype(np.float32), np.sin(twist).astype(np.float32)])
    return tables


def split(x):
    high = x.astype(bf16)
    return high, (x - high.astype(f32)).astype(bf16)


def mm(a, b):
    return jnp.dot(a, b, preferred_element_type=f32)


def kernel(
    sky_ref, sub_ref, cell_ref, ang_ref, seg_ref, waf_ref, mix_ref, knee_ref,
    f1h, f1l, f2h, f2l, f3h, f3l, f4h, f4l, tc_ref, ts_ref,
    out_ref,
    tab, lhs, iqu, local, cosw, sinw, wts, flat, cs, xb, fs, wb,
    vals, av, oh, acc, r1, s2, r2, s3, r3,
    ag_recv, a1_recv, a2_recv, r1_recv, r2_recv, r3_recv,
    ag_send, a1_send, a2_send, r1_send, r2_send, r3_send,
):
    o = lax.axis_index("obs")
    j = lax.axis_index("dt")
    n_obs = lax.axis_size("obs")
    y, z = j // NZ, j % NZ
    before, after = (o + n_obs - 1) % n_obs, (o + 1) % n_obs

    barrier = pltpu.get_barrier_semaphore()
    for other in (before, after):
        pl.semaphore_signal(barrier, inc=1, device_id={"obs": other}, device_id_type=MESH)

    def greet(k, carry):
        pl.semaphore_signal(barrier, inc=1, device_id={"dt": (j + k) % GROUP}, device_id_type=MESH)
        return carry

    lax.fori_loop(1, GROUP, greet, 0)

    double = 2.0 * ang_ref[0]
    cosw[...] = jnp.cos(double)
    sinw[...] = jnp.sin(double)
    local[...] = (sub_ref[0] - o * GROUP) & (n_obs * GROUP - 1)
    keep = jnp.where((seg_ref[...] & 1) == 0, 1.0, 0.0).astype(f32)
    rows = lax.broadcasted_iota(i32, (256, 128), 0)
    bins = (rows & 127) + 128 * lax.broadcasted_iota(i32, (256, 128), 1)
    freq = jnp.minimum(bins, NSAMP - bins).astype(f32)
    lanes = lax.broadcasted_iota(i32, (1, DET), 1)
    knee = knee_ref[...]
    knee_a = jnp.sum(jnp.where(lanes == 2 * j, knee, 0.0), axis=1, keepdims=True)
    knee_b = jnp.sum(jnp.where(lanes == 2 * j + 1, knee, 0.0), axis=1, keepdims=True)
    knees = jnp.where(rows < 128, knee_a, knee_b)
    square = freq * freq
    wts[...] = square / (square + knees * knees)

    pl.semaphore_wait(barrier, GROUP + 1)

    def sky_copy(src, slot, device):
        return pltpu.make_async_remote_copy(
            src_ref=src, dst_ref=tab.at[slot], send_sem=ag_send, recv_sem=ag_recv.at[slot],
            device_id=device, device_id_type=MESH)

    def arrive(slot):
        sky_copy(sky_ref.at[0], slot, {"obs": before}).wait_recv()

    own = sky_ref.at[0]
    for k in range(1, NZ):
        step = (k + 1) // 2 if k % 2 else NZ - k // 2
        sky_copy(own, j, {"dt": y * NZ + (z + step) % NZ}).start()
    for k in range(1, NY):
        sky_copy(own, j, {"dt": (y + k) % NY * NZ + z}).start()
    sky_copy(own, GROUP + j, {"obs": before}).start()
    tab[pl.ds(j, 1)] = sky_ref[...]
    for k in range(1, NZ):
        step = NZ - (k + 1) // 2 if k % 2 else k // 2
        slot = y * NZ + (z + step) % NZ
        arrive(slot)
        for m in range(1, NY):
            sky_copy(tab.at[slot], slot, {"dt": (y + m) % NY * NZ + z}).start()
        sky_copy(tab.at[slot], GROUP + slot, {"obs": before}).start()

    def pass_on(k, carry):
        turn = k // (NY - 1)
        step = jnp.where(turn % 2 == 0, (NZ - turn // 2) % NZ, (turn + 1) // 2)
        slot = (y + 1 + k % (NY - 1)) % NY * NZ + (z + step) % NZ
        arrive(slot)
        sky_copy(tab.at[slot], GROUP + slot, {"obs": before}).start()
        return carry

    lax.fori_loop(0, NZ * (NY - 1), pass_on, 0)

    def await_next(k, carry):
        arrive(GROUP + k)
        return carry

    lax.fori_loop(0, GROUP, await_next, 0)

    for c in range(3):
        high, low = split(tab[:, c, :])
        lhs[c * WINDOW:(c + 1) * WINDOW, :] = high
        lhs[(3 + c) * WINDOW:(4 + c) * WINDOW, :] = low

    def one_hot(row):
        return jnp.where(lax.broadcasted_iota(i32, (PIX, SPAN), 0) == row, 1.0, 0.0).astype(bf16)

    def gather(g, carry):
        base = pl.multiple_of(g * TILE, TILE)
        cells = cell_ref[0, pl.ds(base, TILE), :]
        subs = local[pl.ds(base, TILE), :]
        found = [[], [], []]
        for i in range(TILE):
            result = mm(lhs[...], one_hot(cells[i:i + 1]))
            mask = lax.broadcasted_iota(i32, (WINDOW, SPAN), 0) == subs[i:i + 1]
            for c in range(3):
                both = result[c * WINDOW:(c + 1) * WINDOW] + result[(3 + c) * WINDOW:(4 + c) * WINDOW]
                found[c].append(jnp.sum(jnp.where(mask, both, 0.0), axis=0, keepdims=True))
        for c in range(3):
            iqu[c, pl.ds(base, TILE), :] = jnp.concatenate(found[c], axis=0)
        return carry

    lax.fori_loop(0, DET // TILE, gather, 0)

    tod = keep * (iqu[0] + cosw[...] * iqu[1] + sinw[...] * iqu[2])
    wafer = jnp.broadcast_to(waf_ref[...], (DET, DET)).astype(f32)
    mixing = jnp.where(wafer.T == wafer, mix_ref[0].astype(f32), 0.0).astype(bf16)
    corr = tod + mm(mixing, tod.astype(bf16))
    for h in range(2):
        flat[h] = corr[:, h * 128:(h + 1) * 128]
        for d in range(2):
            cs[:, 2 * d + h, :] = flat[h, pl.ds(d, GROUP, stride=2), :]

    def exchange(src, dst, send, recv):
        def copy(k):
            other = (j + k) % GROUP
            return pltpu.make_async_remote_copy(
                src_ref=src.at[other], dst_ref=dst.at[j], send_sem=send, recv_sem=recv.at[j],
                device_id={"dt": other}, device_id_type=MESH)

        def push(k, carry):
            copy(k).start()
            return carry

        def take(k, carry):
            other = (j + k) % GROUP
            pltpu.make_async_remote_copy(
                src_ref=src.at[other], dst_ref=dst.at[other], send_sem=send, recv_sem=recv.at[other],
                device_id={"dt": other}, device_id_type=MESH).wait_recv()
            return carry

        lax.fori_loop(1, GROUP, push, 0)
        dst[pl.ds(j, 1)] = src[pl.ds(j, 1)]
        lax.fori_loop(1, GROUP, take, 0)

    exchange(cs, xb, a1_send, a1_recv)

    def exact_left(high, low, x):
        xh, xl = split(x)
        return mm(high[...], xh) + (mm(high[...], xl) + mm(low[...], xh))

    def exact_right(x, high, low):
        xh, xl = split(x)
        return mm(xh, high[...]) + (mm(xl, high[...]) + mm(xh, low[...]))

    series = xb[...].reshape(256, 128)
    part = exact_left(f1h, f1l, series)
    re, im = part[:256], part[256:]
    tc, ts = tc_ref[...], ts_ref[...]
    spec = exact_right(jnp.concatenate([re * tc + im * ts, im * tc - re * ts], axis=1), f2h, f2l)
    weight = wts[...]
    spec = spec * jnp.concatenate([weight, weight], axis=1)
    back = exact_right(spec, f3h, f3l)
    re, im = back[:, :128], back[:, 128:]
    turned = jnp.concatenate([re * tc - im * ts, re * ts + im * tc], axis=0)
    fs[...] = exact_left(f4h, f4l, turned).reshape(GROUP, 4, 128)

    exchange(fs, wb, a2_send, a2_recv)

    for d in range(2):
        for h in range(2):
            flat[h, pl.ds(d, GROUP, stride=2), :] = wb[:, 2 * d + h, :]
    weighted = keep * jnp.concatenate([flat[0], flat[1]], axis=1)
    vals[0] = weighted
    vals[1] = weighted * cosw[...]
    vals[2] = weighted * sinw[...]
    acc[...] = jnp.zeros_like(acc)

    def scatter(g, carry):
        base = pl.multiple_of(g * TILE, TILE)
        cells = cell_ref[0, pl.ds(base, TILE), :]
        subs = local[pl.ds(base, TILE), :]
        value = [vals[c, pl.ds(base, TILE), :] for c in range(3)]
        for i in range(TILE):
            span = slice(i * SPAN, (i + 1) * SPAN)
            oh[:, span] = one_hot(cells[i:i + 1])
            mask = lax.broadcasted_iota(i32, (WINDOW, SPAN), 0) == subs[i:i + 1]
            for c in range(3):
                for t, x in enumerate(split(value[c][i:i + 1])):
                    k = 3 * t + c
                    av[k * WINDOW:(k + 1) * WINDOW, span] = jnp.where(mask, x.astype(f32), 0.0).astype(bf16)
        sums = lax.dot_general(av[...], oh[...], (((1,), (1,)), ((), ())), preferred_element_type=f32)
        for c in range(3):
            acc[c] += sums[c * WINDOW:(c + 1) * WINDOW] + sums[(3 + c) * WINDOW:(4 + c) * WINDOW]
        return carry

    lax.fori_loop(0, DET // TILE, scatter, 0)

    def block(row):
        return acc.at[:, pl.ds(pl.multiple_of(row * NZ, NZ), NZ), :]

    def to_next(row):
        return pltpu.make_async_remote_copy(
            src_ref=block(NY + row), dst_ref=r1.at[row], send_sem=r1_send, recv_sem=r1_recv.at[row],
            device_id={"obs": after}, device_id_type=MESH)

    def to_row(row, slot):
        return pltpu.make_async_remote_copy(
            src_ref=s2.at[row], dst_ref=r2.at[slot], send_sem=r2_send, recv_sem=r2_recv.at[slot],
            device_id={"dt": row * NZ + z}, device_id_type=MESH)

    def to_owner(other, slot):
        return pltpu.make_async_remote_copy(
            src_ref=s3.at[other], dst_ref=r3.at[slot], send_sem=r3_send, recv_sem=r3_recv.at[slot],
            device_id={"dt": y * NZ + other}, device_id_type=MESH)

    turns = [(y + k) % NY for k in (2, 1, 3, 0)]
    for row in turns:
        to_next(row).start()
    for k, row in enumerate(turns):
        to_next(row).wait_recv()
        s2[row] = block(row)[...] + r1[row]
        if k < NY - 1:
            to_row(row, y).start()
    total = s2[y]
    for row in turns[:NY - 1]:
        to_row(row, row).wait_recv()
        total = total + r2[row]
    for k in range(NZ):
        s3[k] = total[:, k, :]
    for k in range(NZ - 1):
        step = NZ // 2 + (k + 1) // 2 if k % 2 == 0 else NZ // 2 - (k + 1) // 2
        to_owner((z + step) % NZ, z).start()
    r3[pl.ds(z, 1)] = s3[pl.ds(z, 1)]
    for k in range(1, NZ):
        other = (z + k) % NZ
        to_owner(other, other).wait_recv()
    result = r3[0]
    for k in range(1, NZ):
        result = result + r3[k]
    out_ref[0] = result

    def sky_sent(k, carry):
        sky_copy(own, j, {"obs": before}).wait_send()
        return carry

    lax.fori_loop(0, (NZ - 1) + (NY - 1) + 1 + (NZ - 1) * NY + NZ * (NY - 1), sky_sent, 0)

    def sent(k, carry):
        for src, dst, send, recv in ((cs, xb, a1_send, a1_recv), (fs, wb, a2_send, a2_recv)):
            pltpu.make_async_remote_copy(
                src_ref=src.at[j], dst_ref=dst.at[j], send_sem=send, recv_sem=recv.at[j],
                device_id={"obs": before}, device_id_type=MESH).wait_send()
        return carry

    lax.fori_loop(1, GROUP, sent, 0)
    for row in range(NY):
        to_next(row).wait_send()
    for k in range(1, NY):
        to_row((y + k) % NY, y).wait_send()
    for k in range(1, NZ):
        to_owner((z + k) % NZ, z).wait_send()


def body(sky_map, submap_of, pixel_cell, angles, intervals, wafer_of, mixing, knee):
    vmem = pl.BlockSpec(memory_space=pltpu.VMEM)
    tables = [jnp.asarray(t) for t in dft_tables()]
    args = [sky_map, submap_of, pixel_cell, angles, intervals, wafer_of, mixing, knee, *tables]
    dma = pltpu.SemaphoreType.DMA
    return pl.pallas_call(
        kernel,
        out_shape=jax.ShapeDtypeStruct((1, 3, PIX), f32),
        in_specs=[vmem] * len(args),
        out_specs=vmem,
        scratch_shapes=[
            pltpu.VMEM((WINDOW, 3, PIX), f32),
            pltpu.VMEM((6 * WINDOW, PIX), bf16),
            pltpu.VMEM((3, DET, SPAN), f32),
            pltpu.VMEM((DET, SPAN), i32),
            pltpu.VMEM((DET, SPAN), f32),
            pltpu.VMEM((DET, SPAN), f32),
            pltpu.VMEM((256, 128), f32),
            pltpu.VMEM((2, DET, 128), f32),
            pltpu.VMEM((GROUP, 4, 128), f32),
            pltpu.VMEM((GROUP, 4, 128), f32),
            pltpu.VMEM((GROUP, 4, 128), f32),
            pltpu.VMEM((GROUP, 4, 128), f32),
            pltpu.VMEM((3, DET, SPAN), f32),
            pltpu.VMEM((6 * WINDOW, TILE * SPAN), bf16),
            pltpu.VMEM((PIX, TILE * SPAN), bf16),
            pltpu.VMEM((3, WINDOW, PIX), f32),
            pltpu.VMEM((NY, 3, NZ, PIX), f32),
            pltpu.VMEM((NY, 3, NZ, PIX), f32),
            pltpu.VMEM((NY, 3, NZ, PIX), f32),
            pltpu.VMEM((NZ, 3, PIX), f32),
            pltpu.VMEM((NZ, 3, PIX), f32),
            dma((WINDOW,)), dma((GROUP,)), dma((GROUP,)), dma((NY,)), dma((NY,)), dma((NZ,)),
            dma, dma, dma, dma, dma, dma,
        ],
        compiler_params=pltpu.CompilerParams(
            collective_id=0, has_side_effects=True, vmem_limit_bytes=60 << 20),
        name="mapmaker",
    )(*args)


def solution(mesh):
    return jax.shard_map(
        body,
        mesh=mesh,
        in_specs=(
            P(("obs", "dt"), None, None),
            P("obs", None, "dt"),
            P("obs", None, "dt"),
            P("obs", None, "dt"),
            P("obs", "dt"),
            P("obs", None),
            P("obs", None, None),
            P("obs", None),
        ),
        out_specs=P(("obs", "dt"), None, None),
        check_vma=False,
    )
```

```python
import math

import jax
import jax.numpy as jnp
import ml_dtypes
import numpy as np
from jax import lax
from jax.experimental import pallas as pl
from jax.experimental.pallas import tpu as pltpu
from jax.sharding import PartitionSpec as P

MESH = pl.DeviceIdType.MESH
f32, bf16, i32 = jnp.float32, jnp.bfloat16, jnp.int32

DET = 128
SPAN = 256
PIX = 512
GROUP = 64
NY, NZ = 4, 16
REACH = 4
WINDOW = 2 * GROUP
NSAMP = GROUP * SPAN
TILE = 8


def split_np(x):
    high = x.astype(ml_dtypes.bfloat16)
    low = (x - high.astype(np.float64)).astype(ml_dtypes.bfloat16)
    return high, low


def dft_tables():
    n = 128
    row = np.arange(256)
    row_det, row_n1 = row % 2, 2 * ((row % n) // 2) + row // n
    col_det, col_k1 = row // n, row % n
    same = (row_det[:, None] == col_det[None, :]).astype(np.float64)
    turn = 2.0 * np.pi * ((row_n1[:, None] * col_k1[None, :]) % n) / n
    cos_part, sin_part = same * np.cos(turn), -same * np.sin(turn)
    last = np.concatenate([cos_part, sin_part], axis=1)
    first = np.ascontiguousarray(last.T)
    index = np.arange(n)
    angle = 2.0 * np.pi * ((index[:, None] * index[None, :]) % n) / n
    c, s = np.cos(angle), np.sin(angle)
    forward = np.block([[c, -s], [s, c]])
    backward = np.block([[c, s], [-s, c]]) / NSAMP
    twist = 2.0 * np.pi * (col_k1[:, None] * index[None, :]) / NSAMP
    tables = []
    for x in (first, forward, backward, last):
        tables.extend(split_np(x))
    tables.extend([np.cos(twist).astype(np.float32), np.sin(twist).astype(np.float32)])
    return tables


def split(x):
    high = x.astype(bf16)
    return high, (x - high.astype(f32)).astype(bf16)


def mm(a, b):
    return jnp.dot(a, b, preferred_element_type=f32)


def kernel(
    sky_ref, sub_ref, cell_ref, ang_ref, seg_ref, waf_ref, mix_ref, knee_ref,
    f1h, f1l, f2h, f2l, f3h, f3l, f4h, f4l, tc_ref, ts_ref,
    out_ref,
    tab, lhs, iqu, local, cosw, sinw, wts, cs, xb, fs, wb,
    av, oh, acc, r1, s2, r2, s3, r3,
    ag_recv, a1_recv, a2_recv, r1_recv, r2_recv, r3_recv,
    ag_send, a1_send, a2_send, r1_send, r2_send, r3_send,
):
    o = lax.axis_index("obs")
    j = lax.axis_index("dt")
    n_obs = lax.axis_size("obs")
    y, z = j >> 4, j & (NZ - 1)
    before, after = (o + n_obs - 1) & (n_obs - 1), (o + 1) & (n_obs - 1)

    def chip(dy, dz):
        return ((y + dy) & (NY - 1)) * NZ + ((z + dz) & (NZ - 1))

    barrier = pltpu.get_barrier_semaphore()
    near = [chip(0, s) for s in range(-REACH, REACH + 1) if s] + [chip(s, 0) for s in range(1, NY)]
    for other in near:
        pl.semaphore_signal(barrier, inc=1, device_id={"dt": other}, device_id_type=MESH)
    for other in (before, after):
        pl.semaphore_signal(barrier, inc=1, device_id={"obs": other}, device_id_type=MESH)

    double = 2.0 * ang_ref[0]
    cosw[...] = jnp.cos(double)
    sinw[...] = jnp.sin(double)
    local[...] = (sub_ref[0] - o * GROUP) & (n_obs * GROUP - 1)
    keep = jnp.where((seg_ref[...] & 1) == 0, 1.0, 0.0).astype(f32)
    rows = lax.broadcasted_iota(i32, (256, 128), 0)
    bins = (rows & 127) + 128 * lax.broadcasted_iota(i32, (256, 128), 1)
    freq = jnp.minimum(bins, NSAMP - bins).astype(f32)
    lanes = lax.broadcasted_iota(i32, (1, DET), 1)
    knee = knee_ref[...]
    knee_a = jnp.sum(jnp.where(lanes == 2 * j, knee, 0.0), axis=1, keepdims=True)
    knee_b = jnp.sum(jnp.where(lanes == 2 * j + 1, knee, 0.0), axis=1, keepdims=True)
    knees = jnp.where(rows < 128, knee_a, knee_b)
    square = freq * freq
    wts[...] = square / (square + knees * knees)

    pl.semaphore_wait(barrier, len(near) + 2)

    def sky_copy(src, slot, device):
        return pltpu.make_async_remote_copy(
            src_ref=src, dst_ref=tab.at[slot], send_sem=ag_send, recv_sem=ag_recv.at[slot],
            device_id=device, device_id_type=MESH)

    own = sky_ref

    def send(slot, device):
        sky_copy(tab.at[slot], slot, device).start()

    def to_before(slot):
        sky_copy(tab.at[slot], GROUP + slot, {"obs": before}).start()

    def arrive(slot):
        sky_copy(own, slot, {"obs": before}).wait_recv()

    for s in range(REACH, 0, -1):
        for step in (s, -s):
            sky_copy(own, j, {"dt": chip(0, step)}).start()
    for step in (1, -1):
        sky_copy(own, j, {"dt": chip(step, 0)}).start()
    sky_copy(own, GROUP + j, {"obs": before}).start()
    tab[pl.ds(j, 1)] = sky_ref[...][None]
    sky_sends = 2 * REACH + 3
    for s in range(1, NZ // 2 + 1):
        for sign in (1, -1) if s < NZ // 2 else (1,):
            slot = chip(0, -sign * s)
            arrive(slot)
            if s == REACH:
                for far in range(REACH if sign == 1 else REACH - 1, 0, -1):
                    send(slot, {"dt": chip(0, sign * far)})
                    sky_sends += 1
            send(slot, {"dt": chip(1, 0)})
            send(slot, {"dt": chip(-1, 0)})
            to_before(slot)
            sky_sends += 3

    def offset(k):
        return jnp.where((k & 1) == 1, -((k + 1) >> 1), k >> 1)

    def pass_on(k, carry):
        dz = offset(k)
        odd = (z + dz) & 1
        low, high = chip(-1, dz), chip(1, dz)
        arrive(low)
        arrive(high)
        send(chip(2 * odd - 1, dz), {"dt": chip(1 - 2 * odd, 0)})
        to_before(low)
        to_before(high)
        return carry

    lax.fori_loop(0, NZ, pass_on, 0)

    def pass_last(k, carry):
        slot = chip(2, offset(k))
        arrive(slot)
        to_before(slot)
        return carry

    lax.fori_loop(0, NZ, pass_last, 0)
    sky_sends += 4 * NZ

    def await_next(k, carry):
        arrive(GROUP + k)
        return carry

    lax.fori_loop(0, GROUP, await_next, 0)

    for c in range(3):
        high, low = split(tab[:, c, 0, :])
        lhs[c * WINDOW:(c + 1) * WINDOW, :] = high
        lhs[(3 + c) * WINDOW:(4 + c) * WINDOW, :] = low

    def one_hot(row):
        return jnp.where(lax.broadcasted_iota(i32, (PIX, SPAN), 0) == row, 1.0, 0.0).astype(bf16)

    def gather(g, carry):
        base = pl.multiple_of(g * TILE, TILE)
        cells = cell_ref[0, pl.ds(base, TILE), :]
        subs = local[pl.ds(base, TILE), :]
        found = [[], [], []]
        for i in range(TILE):
            result = mm(lhs[...], one_hot(cells[i:i + 1]))
            mask = lax.broadcasted_iota(i32, (WINDOW, SPAN), 0) == subs[i:i + 1]
            for c in range(3):
                both = result[c * WINDOW:(c + 1) * WINDOW] + result[(3 + c) * WINDOW:(4 + c) * WINDOW]
                found[c].append(jnp.sum(jnp.where(mask, both, 0.0), axis=0, keepdims=True))
        for c in range(3):
            iqu[c, pl.ds(base, TILE), :] = jnp.concatenate(found[c], axis=0)
        return carry

    lax.fori_loop(0, DET // TILE, gather, 0)

    tod = keep * (iqu[0] + cosw[...] * iqu[1] + sinw[...] * iqu[2])
    wafer = jnp.broadcast_to(waf_ref[...], (DET, DET)).astype(f32)
    mixing = jnp.where(wafer.T == wafer, mix_ref[0].astype(f32), 0.0).astype(bf16)
    corr = tod + mm(mixing, tod.astype(bf16))
    for i in range(GROUP):
        cs[i] = corr[2 * i:2 * i + 2]

    def piece(src, dst, send_sem, recv_sem, here, there, device):
        return pltpu.make_async_remote_copy(
            src_ref=src.at[here], dst_ref=dst.at[there], send_sem=send_sem, recv_sem=recv_sem.at[there],
            device_id={"dt": device}, device_id_type=MESH)

    def spread(src, dst, send_sem, recv_sem):
        def push(k, carry):
            other = (j + k) & (GROUP - 1)
            piece(src, dst, send_sem, recv_sem, other, j, other).start()
            return carry

        lax.fori_loop(1, GROUP, push, 0)
        dst[pl.ds(j, 1)] = src[pl.ds(j, 1)]

    def take(src, dst, send_sem, recv_sem, source):
        piece(src, dst, send_sem, recv_sem, source, source, source).wait_recv()

    spread(cs, xb, a1_send, a1_recv)

    def take_series(k, carry):
        take(cs, xb, a1_send, a1_recv, (j + k) & (GROUP - 1))
        return carry

    lax.fori_loop(1, GROUP, take_series, 0)

    def exact_left(high, low, x):
        xh, xl = split(x)
        return mm(high[...], xh) + (mm(high[...], xl) + mm(low[...], xh))

    def exact_right(x, high, low):
        xh, xl = split(x)
        return mm(xh, high[...]) + (mm(xl, high[...]) + mm(xh, low[...]))

    pairs = jnp.concatenate([xb[i] for i in range(GROUP)], axis=0)
    series = jnp.concatenate([pairs[:, :128], pairs[:, 128:]], axis=0)
    part = exact_left(f1h, f1l, series)
    re, im = part[:256], part[256:]
    tc, ts = tc_ref[...], ts_ref[...]
    spec = exact_right(jnp.concatenate([re * tc + im * ts, im * tc - re * ts], axis=1), f2h, f2l)
    weight = wts[...]
    spec = spec * jnp.concatenate([weight, weight], axis=1)
    back = exact_right(spec, f3h, f3l)
    re, im = back[:, :128], back[:, 128:]
    turned = jnp.concatenate([re * tc - im * ts, re * ts + im * tc], axis=0)
    filtered = exact_left(f4h, f4l, turned)
    filtered = jnp.concatenate([filtered[:128], filtered[128:]], axis=1)
    for i in range(GROUP):
        fs[i] = filtered[2 * i:2 * i + 2]
    spread(fs, wb, a2_send, a2_recv)

    acc[...] = jnp.zeros_like(acc)

    def scatter(k, carry):
        dq = k >> 2
        g = ((y + k) & (NY - 1)) * 4 + (((z >> 2) + jnp.where(dq >= 2, 5 - dq, dq)) & 3)
        for i in range(TILE // 2):
            source = g * (TILE // 2) + i

            @pl.when(source != j)
            def _():
                take(fs, wb, a2_send, a2_recv, source)

        base = pl.multiple_of(g * TILE, TILE)
        cells = cell_ref[0, pl.ds(base, TILE), :]
        subs = local[pl.ds(base, TILE), :]
        weighted = jnp.concatenate([wb[g * (TILE // 2) + i] for i in range(TILE // 2)], axis=0) * keep
        value = [weighted, weighted * cosw[pl.ds(base, TILE), :], weighted * sinw[pl.ds(base, TILE), :]]
        for i in range(TILE):
            span = slice(i * SPAN, (i + 1) * SPAN)
            oh[:, span] = one_hot(cells[i:i + 1])
            mask = lax.broadcasted_iota(i32, (WINDOW, SPAN), 0) == subs[i:i + 1]
            for c in range(3):
                for t, x in enumerate(split(value[c][i:i + 1])):
                    k = 3 * t + c
                    av[k * WINDOW:(k + 1) * WINDOW, span] = jnp.where(mask, x.astype(f32), 0.0).astype(bf16)
        sums = lax.dot_general(av[...], oh[...], (((1,), (1,)), ((), ())), preferred_element_type=f32)
        for c in range(3):
            acc[c] += sums[c * WINDOW:(c + 1) * WINDOW] + sums[(3 + c) * WINDOW:(4 + c) * WINDOW]
        return carry

    lax.fori_loop(0, DET // TILE, scatter, 0)

    def block(row):
        return acc.at[:, pl.ds(pl.multiple_of(row * NZ, NZ), NZ), :]

    def to_next(row):
        return pltpu.make_async_remote_copy(
            src_ref=block(NY + row), dst_ref=r1.at[row], send_sem=r1_send, recv_sem=r1_recv.at[row],
            device_id={"obs": after}, device_id_type=MESH)

    def to_row(row, slot):
        return pltpu.make_async_remote_copy(
            src_ref=s2.at[row], dst_ref=r2.at[slot], send_sem=r2_send, recv_sem=r2_recv.at[slot],
            device_id={"dt": row * NZ + z}, device_id_type=MESH)

    def to_owner(other, slot):
        return pltpu.make_async_remote_copy(
            src_ref=s3.at[other], dst_ref=r3.at[slot], send_sem=r3_send, recv_sem=r3_recv.at[slot],
            device_id={"dt": y * NZ + other}, device_id_type=MESH)

    turns = [(y + k) & (NY - 1) for k in (2, 1, 3, 0)]
    for row in turns:
        to_next(row).start()
    for k, row in enumerate(turns):
        to_next(row).wait_recv()
        s2[row] = block(row)[...] + r1[row]
        if k < NY - 1:
            to_row(row, y).start()
    total = s2[y]
    for row in turns[:NY - 1]:
        to_row(row, row).wait_recv()
        total = total + r2[row]
    for k in range(NZ):
        s3[k] = total[:, k, :]
    for k in range(NZ - 1):
        step = NZ // 2 + (k + 1) // 2 if k % 2 == 0 else NZ // 2 - (k + 1) // 2
        to_owner((z + step) & (NZ - 1), z).start()
    r3[pl.ds(z, 1)] = s3[pl.ds(z, 1)]
    for k in range(1, NZ):
        other = (z + k) & (NZ - 1)
        to_owner(other, other).wait_recv()
    result = r3[0]
    for k in range(1, NZ):
        result = result + r3[k]
    out_ref[...] = result[:, None, :]

    def sky_sent(k, carry):
        sky_copy(own, j, {"obs": before}).wait_send()
        return carry

    lax.fori_loop(0, sky_sends, sky_sent, 0)

    def sent(k, carry):
        for src, dst, send, recv in ((cs, xb, a1_send, a1_recv), (fs, wb, a2_send, a2_recv)):
            pltpu.make_async_remote_copy(
                src_ref=src.at[j], dst_ref=dst.at[j], send_sem=send, recv_sem=recv.at[j],
                device_id={"obs": before}, device_id_type=MESH).wait_send()
        return carry

    lax.fori_loop(1, GROUP, sent, 0)
    for row in range(NY):
        to_next(row).wait_send()
    for k in range(1, NY):
        to_row((y + k) & (NY - 1), y).wait_send()
    for k in range(1, NZ):
        to_owner((z + k) & (NZ - 1), z).wait_send()


def body(sky_map, submap_of, pixel_cell, angles, intervals, wafer_of, mixing, knee):
    vmem = pl.BlockSpec(memory_space=pltpu.VMEM)
    tables = [jnp.asarray(t) for t in dft_tables()]
    args = [jnp.transpose(sky_map, (1, 0, 2)), submap_of, pixel_cell, angles, intervals, wafer_of, mixing, knee, *tables]
    dma = pltpu.SemaphoreType.DMA
    result = pl.pallas_call(
        kernel,
        out_shape=jax.ShapeDtypeStruct((3, 1, PIX), f32),
        in_specs=[vmem] * len(args),
        out_specs=vmem,
        scratch_shapes=[
            pltpu.VMEM((WINDOW, 3, 1, PIX), f32),
            pltpu.VMEM((6 * WINDOW, PIX), bf16),
            pltpu.VMEM((3, DET, SPAN), f32),
            pltpu.VMEM((DET, SPAN), i32),
            pltpu.VMEM((DET, SPAN), f32),
            pltpu.VMEM((DET, SPAN), f32),
            pltpu.VMEM((256, 128), f32),
            pltpu.VMEM((GROUP, 2, SPAN), f32),
            pltpu.VMEM((GROUP, 2, SPAN), f32),
            pltpu.VMEM((GROUP, 2, SPAN), f32),
            pltpu.VMEM((GROUP, 2, SPAN), f32),
            pltpu.VMEM((6 * WINDOW, TILE * SPAN), bf16),
            pltpu.VMEM((PIX, TILE * SPAN), bf16),
            pltpu.VMEM((3, WINDOW, PIX), f32),
            pltpu.VMEM((NY, 3, NZ, PIX), f32),
            pltpu.VMEM((NY, 3, NZ, PIX), f32),
            pltpu.VMEM((NY, 3, NZ, PIX), f32),
            pltpu.VMEM((NZ, 3, PIX), f32),
            pltpu.VMEM((NZ, 3, PIX), f32),
            dma((WINDOW,)), dma((GROUP,)), dma((GROUP,)), dma((NY,)), dma((NY,)), dma((NZ,)),
            dma, dma, dma, dma, dma, dma,
        ],
        compiler_params=pltpu.CompilerParams(
            collective_id=0, has_side_effects=True, vmem_limit_bytes=60 << 20),
        name="mapmaker",
    )(*args)
    return jnp.transpose(result, (1, 0, 2))


def solution(mesh):
    return jax.shard_map(
        body,
        mesh=mesh,
        in_specs=(
            P(("obs", "dt"), None, None),
            P("obs", None, "dt"),
            P("obs", None, "dt"),
            P("obs", None, "dt"),
            P("obs", "dt"),
            P("obs", None),
            P("obs", None, None),
            P("obs", None),
        ),
        out_specs=P(("obs", "dt"), None, None),
        check_vma=False,
    )
```

```python
import math

import jax
import jax.numpy as jnp
import ml_dtypes
import numpy as np
from jax import lax
from jax.experimental import pallas as pl
from jax.experimental.pallas import tpu as pltpu
from jax.sharding import PartitionSpec as P

MESH = pl.DeviceIdType.MESH
f32, bf16, i32 = jnp.float32, jnp.bfloat16, jnp.int32

DET = 128
SPAN = 256
PIX = 512
GROUP = 64
NY, NZ = 4, 16
REACH = 4
LAG = 3
WINDOW = 2 * GROUP
NSAMP = GROUP * SPAN
TILE = 8


def split_np(x):
    high = x.astype(ml_dtypes.bfloat16)
    low = (x - high.astype(np.float64)).astype(ml_dtypes.bfloat16)
    return high, low


def dft_tables():
    n = 128
    row = np.arange(256)
    row_det, row_n1 = row % 2, 2 * ((row % n) // 2) + row // n
    col_det, col_k1 = row // n, row % n
    same = (row_det[:, None] == col_det[None, :]).astype(np.float64)
    turn = 2.0 * np.pi * ((row_n1[:, None] * col_k1[None, :]) % n) / n
    cos_part, sin_part = same * np.cos(turn), -same * np.sin(turn)
    last = np.concatenate([cos_part, sin_part], axis=1)
    first = np.ascontiguousarray(last.T)
    index = np.arange(n)
    angle = 2.0 * np.pi * ((index[:, None] * index[None, :]) % n) / n
    c, s = np.cos(angle), np.sin(angle)
    forward = np.block([[c, -s], [s, c]])
    backward = np.block([[c, s], [-s, c]]) / NSAMP
    twist = 2.0 * np.pi * (col_k1[:, None] * index[None, :]) / NSAMP
    tables = []
    for x in (first, forward, backward, last):
        tables.extend(split_np(x))
    tables.extend([np.cos(twist).astype(np.float32), np.sin(twist).astype(np.float32)])
    return tables


def split(x):
    high = x.astype(bf16)
    return high, (x - high.astype(f32)).astype(bf16)


def mm(a, b):
    return jnp.dot(a, b, preferred_element_type=f32)


INPUTS = 17


def kernel(sky_ref, *refs):
    held, refs = refs[:INPUTS], refs[INPUTS:]
    out_ref, refs = refs[0], refs[1:]
    local_copies, refs = refs[:INPUTS], refs[INPUTS:]
    (
        sub_ref, cell_ref, ang_ref, seg_ref, waf_ref, mix_ref, knee_ref,
        f1h, f1l, f2h, f2l, f3h, f3l, f4h, f4l, tc_ref, ts_ref,
    ) = local_copies
    (
        in_sem,
        tab, lhs, iqu, local, cosw, sinw, wts, cs, xb, fs, wb,
        av, oh, acc, r1, s2, r2, s3, r3,
        ag_recv, a1_recv, a2_recv, r1_recv, r2_recv, r3_recv,
        ag_send, a1_send, a2_send, r1_send, r2_send, r3_send,
    ) = refs
    o = lax.axis_index("obs")
    j = lax.axis_index("dt")
    n_obs = lax.axis_size("obs")
    y, z = j >> 4, j & (NZ - 1)
    before, after = (o + n_obs - 1) & (n_obs - 1), (o + 1) & (n_obs - 1)

    def chip(dy, dz):
        return ((y + dy) & (NY - 1)) * NZ + ((z + dz) & (NZ - 1))

    barrier = pltpu.get_barrier_semaphore()
    near = [chip(0, s) for s in range(-REACH, REACH + 1) if s] + [chip(s, 0) for s in range(1, NY)]
    for other in near:
        pl.semaphore_signal(barrier, inc=1, device_id={"dt": other}, device_id_type=MESH)
    for other in (before, after):
        pl.semaphore_signal(barrier, inc=1, device_id={"obs": other}, device_id_type=MESH)

    def load(k):
        return pltpu.make_async_copy(held[k], local_copies[k], in_sem.at[k])

    own_block = pltpu.make_async_copy(sky_ref, tab.at[j], in_sem.at[INPUTS])
    early, late = (2, 0, 3, 6), (1, 4, 5, *range(7, INPUTS))
    for k in (*early, *late):
        load(k).start()
    own_block.start()
    acc[...] = jnp.zeros_like(acc)
    for k in early:
        load(k).wait()

    double = 2.0 * ang_ref[0]
    cosw[...] = jnp.cos(double)
    sinw[...] = jnp.sin(double)
    local[...] = (sub_ref[0] - o * GROUP) & (n_obs * GROUP - 1)
    keep = jnp.where((seg_ref[...] & 1) == 0, 1.0, 0.0).astype(f32)
    rows = lax.broadcasted_iota(i32, (256, 128), 0)
    bins = (rows & 127) + 128 * lax.broadcasted_iota(i32, (256, 128), 1)
    freq = jnp.minimum(bins, NSAMP - bins).astype(f32)
    lanes = lax.broadcasted_iota(i32, (1, DET), 1)
    knee = knee_ref[...]
    knee_a = jnp.sum(jnp.where(lanes == 2 * j, knee, 0.0), axis=1, keepdims=True)
    knee_b = jnp.sum(jnp.where(lanes == 2 * j + 1, knee, 0.0), axis=1, keepdims=True)
    knees = jnp.where(rows < 128, knee_a, knee_b)
    square = freq * freq
    wts[...] = square / (square + knees * knees)

    pl.semaphore_wait(barrier, len(near) + 2)

    def sky_copy(src, slot, device):
        return pltpu.make_async_remote_copy(
            src_ref=src, dst_ref=tab.at[slot], send_sem=ag_send, recv_sem=ag_recv.at[slot],
            device_id=device, device_id_type=MESH)

    own = sky_ref

    def send(slot, device):
        sky_copy(tab.at[slot], slot, device).start()

    def to_before(slot):
        sky_copy(tab.at[slot], GROUP + slot, {"obs": before}).start()

    def arrive(slot):
        sky_copy(own, slot, {"obs": before}).wait_recv()

    for s in range(REACH, 0, -1):
        for step in (s, -s):
            sky_copy(own, j, {"dt": chip(0, step)}).start()
    for step in (2, 1, -1):
        sky_copy(own, j, {"dt": chip(step, 0)}).start()
    sky_copy(own, GROUP + j, {"obs": before}).start()
    sky_sends = 2 * REACH + NY

    def signs(s):
        return (1, -1) if 0 < s < NZ // 2 else (1,)

    def from_rows(s):
        for sign in signs(s):
            for dy in (1, -1, 2):
                slot = chip(dy, -sign * s)
                arrive(slot)
                to_before(slot)

    for s in range(1, NZ // 2 + 1):
        for sign in signs(s):
            slot = chip(0, -sign * s)
            arrive(slot)
            if s == REACH:
                for far in range(REACH if sign == 1 else REACH - 1, 0, -1):
                    send(slot, {"dt": chip(0, sign * far)})
                    sky_sends += 1
            for dy in (2, 1, -1):
                send(slot, {"dt": chip(dy, 0)})
            to_before(slot)
            sky_sends += NY
        if s >= LAG:
            from_rows(s - LAG)
    for s in range(NZ // 2 + 1 - LAG, NZ // 2 + 1):
        from_rows(s)
    sky_sends += NZ * (NY - 1)

    def prepare(first):
        for c in range(3):
            high, low = split(tab[first:first + GROUP, c, 0, :])
            row = c * WINDOW + first
            lhs[row:row + GROUP, :] = high
            lhs[3 * WINDOW + row:3 * WINDOW + row + GROUP, :] = low

    own_block.wait()
    prepare(0)

    def await_next(k, carry):
        arrive(GROUP + k)
        return carry

    lax.fori_loop(0, GROUP, await_next, 0)

    prepare(GROUP)
    for k in late:
        load(k).wait()

    def one_hot(row):
        return jnp.where(lax.broadcasted_iota(i32, (PIX, SPAN), 0) == row, 1.0, 0.0).astype(bf16)

    def gather(g, carry):
        base = pl.multiple_of(g * TILE, TILE)
        cells = cell_ref[0, pl.ds(base, TILE), :]
        subs = local[pl.ds(base, TILE), :]
        found = [[], [], []]
        for i in range(TILE):
            result = mm(lhs[...], one_hot(cells[i:i + 1]))
            mask = lax.broadcasted_iota(i32, (WINDOW, SPAN), 0) == subs[i:i + 1]
            for c in range(3):
                both = result[c * WINDOW:(c + 1) * WINDOW] + result[(3 + c) * WINDOW:(4 + c) * WINDOW]
                found[c].append(jnp.sum(jnp.where(mask, both, 0.0), axis=0, keepdims=True))
        for c in range(3):
            iqu[c, pl.ds(base, TILE), :] = jnp.concatenate(found[c], axis=0)
        return carry

    lax.fori_loop(0, DET // TILE, gather, 0)

    tod = keep * (iqu[0] + cosw[...] * iqu[1] + sinw[...] * iqu[2])
    wafer = jnp.broadcast_to(waf_ref[...], (DET, DET)).astype(f32)
    mixing = jnp.where(wafer.T == wafer, mix_ref[0].astype(f32), 0.0).astype(bf16)
    corr = tod + mm(mixing, tod.astype(bf16))
    for i in range(GROUP):
        cs[i] = corr[2 * i:2 * i + 2]

    def piece(src, dst, send_sem, recv_sem, here, there, device):
        return pltpu.make_async_remote_copy(
            src_ref=src.at[here], dst_ref=dst.at[there], send_sem=send_sem, recv_sem=recv_sem.at[there],
            device_id={"dt": device}, device_id_type=MESH)

    def spread(src, dst, send_sem, recv_sem):
        def push(k, carry):
            other = (j + k) & (GROUP - 1)
            piece(src, dst, send_sem, recv_sem, other, j, other).start()
            return carry

        lax.fori_loop(1, GROUP, push, 0)
        dst[pl.ds(j, 1)] = src[pl.ds(j, 1)]

    def take(src, dst, send_sem, recv_sem, source):
        piece(src, dst, send_sem, recv_sem, source, source, source).wait_recv()

    def all_left(src, send_sem, dst, recv_sem):
        def left(k, carry):
            piece(src, dst, send_sem, recv_sem, j, j, (j + 1) & (GROUP - 1)).wait_send()
            return carry

        lax.fori_loop(1, GROUP, left, 0)

    spread(cs, xb, a1_send, a1_recv)

    def sky_left(k, carry):
        sky_copy(own, j, {"obs": before}).wait_send()
        return carry

    lax.fori_loop(0, sky_sends, sky_left, 0)

    def take_series(k, carry):
        take(cs, xb, a1_send, a1_recv, (j + k) & (GROUP - 1))
        return carry

    lax.fori_loop(1, GROUP, take_series, 0)

    def exact_left(high, low, x):
        xh, xl = split(x)
        return mm(high[...], xh) + (mm(high[...], xl) + mm(low[...], xh))

    def exact_right(x, high, low):
        xh, xl = split(x)
        return mm(xh, high[...]) + (mm(xl, high[...]) + mm(xh, low[...]))

    pairs = jnp.concatenate([xb[i] for i in range(GROUP)], axis=0)
    series = jnp.concatenate([pairs[:, :128], pairs[:, 128:]], axis=0)
    part = exact_left(f1h, f1l, series)
    re, im = part[:256], part[256:]
    tc, ts = tc_ref[...], ts_ref[...]
    spec = exact_right(jnp.concatenate([re * tc + im * ts, im * tc - re * ts], axis=1), f2h, f2l)
    weight = wts[...]
    spec = spec * jnp.concatenate([weight, weight], axis=1)
    back = exact_right(spec, f3h, f3l)
    re, im = back[:, :128], back[:, 128:]
    turned = jnp.concatenate([re * tc - im * ts, re * ts + im * tc], axis=0)
    filtered = exact_left(f4h, f4l, turned)
    filtered = jnp.concatenate([filtered[:128], filtered[128:]], axis=1)
    for i in range(GROUP):
        fs[i] = filtered[2 * i:2 * i + 2]
    spread(fs, wb, a2_send, a2_recv)
    all_left(cs, a1_send, xb, a1_recv)

    def scatter(k, carry):
        dq = k >> 2
        g = ((y + k) & (NY - 1)) * 4 + (((z >> 2) + jnp.where(dq >= 2, 5 - dq, dq)) & 3)
        for i in range(TILE // 2):
            source = g * (TILE // 2) + i

            @pl.when(source != j)
            def _():
                take(fs, wb, a2_send, a2_recv, source)

        base = pl.multiple_of(g * TILE, TILE)
        cells = cell_ref[0, pl.ds(base, TILE), :]
        subs = local[pl.ds(base, TILE), :]
        weighted = jnp.concatenate([wb[g * (TILE // 2) + i] for i in range(TILE // 2)], axis=0) * keep
        value = [weighted, weighted * cosw[pl.ds(base, TILE), :], weighted * sinw[pl.ds(base, TILE), :]]
        for i in range(TILE):
            span = slice(i * SPAN, (i + 1) * SPAN)
            oh[:, span] = one_hot(cells[i:i + 1])
            mask = lax.broadcasted_iota(i32, (WINDOW, SPAN), 0) == subs[i:i + 1]
            for c in range(3):
                for t, x in enumerate(split(value[c][i:i + 1])):
                    k = 3 * t + c
                    av[k * WINDOW:(k + 1) * WINDOW, span] = jnp.where(mask, x.astype(f32), 0.0).astype(bf16)
        sums = lax.dot_general(av[...], oh[...], (((1,), (1,)), ((), ())), preferred_element_type=f32)
        for c in range(3):
            acc[c] += sums[c * WINDOW:(c + 1) * WINDOW] + sums[(3 + c) * WINDOW:(4 + c) * WINDOW]
        return carry

    lax.fori_loop(0, DET // TILE, scatter, 0)

    half = NZ // 2
    far_half = 1 - (z >> 3)
    halves = (far_half, 1 - far_half)

    def block(row, part):
        return acc.at[:, pl.ds(pl.multiple_of(row * NZ + part * half, half), half), :]

    def to_next(row, part):
        return pltpu.make_async_remote_copy(
            src_ref=block(NY + row, part), dst_ref=r1.at[part, row], send_sem=r1_send,
            recv_sem=r1_recv.at[part, row], device_id={"obs": after}, device_id_type=MESH)

    def to_row(row, part, slot):
        return pltpu.make_async_remote_copy(
            src_ref=s2.at[part, row], dst_ref=r2.at[part, slot], send_sem=r2_send,
            recv_sem=r2_recv.at[part, slot], device_id={"dt": row * NZ + z}, device_id_type=MESH)

    def to_owner(other, slot):
        return pltpu.make_async_remote_copy(
            src_ref=s3.at[other], dst_ref=r3.at[slot], send_sem=r3_send, recv_sem=r3_recv.at[slot],
            device_id={"dt": y * NZ + other}, device_id_type=MESH)

    turns = [(y + k) & (NY - 1) for k in (2, 1, 3, 0)]
    for part in halves:
        for row in turns:
            to_next(row, part).start()
    for part in halves:
        for k, row in enumerate(turns):
            to_next(row, part).wait_recv()
            s2[part, row] = block(row, part)[...] + r1[part, row]
            if k < NY - 1:
                to_row(row, part, y).start()
    for part in halves:
        total = s2[part, y]
        for row in turns[:NY - 1]:
            to_row(row, part, row).wait_recv()
            total = total + r2[part, row]
        for k in range(half):
            other = part * half + k
            s3[other] = total[:, k, :]

            @pl.when(other != z)
            def _():
                to_owner(other, z).start()

    r3[pl.ds(z, 1)] = s3[pl.ds(z, 1)]
    for k in range(1, NZ):
        other = (z + k) & (NZ - 1)
        to_owner(other, other).wait_recv()
    result = r3[0]
    for k in range(1, NZ):
        result = result + r3[k]
    out_ref[...] = result[:, None, :]

    all_left(fs, a2_send, wb, a2_recv)
    for part in range(2):
        for row in range(NY):
            to_next(row, part).wait_send()
        for k in range(1, NY):
            to_row((y + k) & (NY - 1), part, y).wait_send()
    for k in range(1, NZ):
        to_owner((z + k) & (NZ - 1), z).wait_send()


def body(sky_map, submap_of, pixel_cell, angles, intervals, wafer_of, mixing, knee):
    vmem = pl.BlockSpec(memory_space=pltpu.VMEM)
    tables = [jnp.asarray(t) for t in dft_tables()]
    args = [jnp.transpose(sky_map, (1, 0, 2)), submap_of, pixel_cell, angles, intervals, wafer_of, mixing, knee, *tables]
    dma = pltpu.SemaphoreType.DMA
    result = pl.pallas_call(
        kernel,
        out_shape=jax.ShapeDtypeStruct((3, 1, PIX), f32),
        in_specs=[pl.BlockSpec(memory_space=pl.ANY)] * len(args),
        out_specs=vmem,
        scratch_shapes=[
            *[pltpu.VMEM(a.shape, a.dtype) for a in args[1:]],
            dma((INPUTS + 1,)),
            pltpu.VMEM((WINDOW, 3, 1, PIX), f32),
            pltpu.VMEM((6 * WINDOW, PIX), bf16),
            pltpu.VMEM((3, DET, SPAN), f32),
            pltpu.VMEM((DET, SPAN), i32),
            pltpu.VMEM((DET, SPAN), f32),
            pltpu.VMEM((DET, SPAN), f32),
            pltpu.VMEM((256, 128), f32),
            pltpu.VMEM((GROUP, 2, SPAN), f32),
            pltpu.VMEM((GROUP, 2, SPAN), f32),
            pltpu.VMEM((GROUP, 2, SPAN), f32),
            pltpu.VMEM((GROUP, 2, SPAN), f32),
            pltpu.VMEM((6 * WINDOW, TILE * SPAN), bf16),
            pltpu.VMEM((PIX, TILE * SPAN), bf16),
            pltpu.VMEM((3, WINDOW, PIX), f32),
            pltpu.VMEM((2, NY, 3, NZ // 2, PIX), f32),
            pltpu.VMEM((2, NY, 3, NZ // 2, PIX), f32),
            pltpu.VMEM((2, NY, 3, NZ // 2, PIX), f32),
            pltpu.VMEM((NZ, 3, PIX), f32),
            pltpu.VMEM((NZ, 3, PIX), f32),
            dma((WINDOW,)), dma((GROUP,)), dma((GROUP,)), dma((2, NY)), dma((2, NY)), dma((NZ,)),
            dma, dma, dma, dma, dma, dma,
        ],
        compiler_params=pltpu.CompilerParams(
            collective_id=0, has_side_effects=True, vmem_limit_bytes=60 << 20),
        name="mapmaker",
    )(*args)
    return jnp.transpose(result, (1, 0, 2))


def solution(mesh):
    return jax.shard_map(
        body,
        mesh=mesh,
        in_specs=(
            P(("obs", "dt"), None, None),
            P("obs", None, "dt"),
            P("obs", None, "dt"),
            P("obs", None, "dt"),
            P("obs", "dt"),
            P("obs", None),
            P("obs", None, None),
            P("obs", None),
        ),
        out_specs=P(("obs", "dt"), None, None),
        check_vma=False,
    )
```

```python
import math

import jax
import jax.numpy as jnp
import ml_dtypes
import numpy as np
from jax import lax
from jax.experimental import pallas as pl
from jax.experimental.pallas import tpu as pltpu
from jax.sharding import PartitionSpec as P

MESH = pl.DeviceIdType.MESH
f32, bf16, i32 = jnp.float32, jnp.bfloat16, jnp.int32

DET = 128
SPAN = 256
PIX = 512
GROUP = 64
NY, NZ = 4, 16
REACH = 4
LAG = 3
WINDOW = 2 * GROUP
NSAMP = GROUP * SPAN
TILE = 8


def split_np(x):
    high = x.astype(ml_dtypes.bfloat16)
    low = (x - high.astype(np.float64)).astype(ml_dtypes.bfloat16)
    return high, low


def dft_tables():
    n = 128
    row = np.arange(256)
    row_det, row_n1 = row % 2, 2 * ((row % n) // 2) + row // n
    col_det, col_k1 = row // n, row % n
    same = (row_det[:, None] == col_det[None, :]).astype(np.float64)
    turn = 2.0 * np.pi * ((row_n1[:, None] * col_k1[None, :]) % n) / n
    cos_part, sin_part = same * np.cos(turn), -same * np.sin(turn)
    last = np.concatenate([cos_part, sin_part], axis=1)
    first = np.ascontiguousarray(last.T)
    index = np.arange(n)
    angle = 2.0 * np.pi * ((index[:, None] * index[None, :]) % n) / n
    c, s = np.cos(angle), np.sin(angle)
    forward = np.block([[c, -s], [s, c]])
    backward = np.block([[c, s], [-s, c]]) / NSAMP
    twist = 2.0 * np.pi * (col_k1[:, None] * index[None, :]) / NSAMP
    tables = []
    for x in (first, forward, backward, last):
        tables.extend(split_np(x))
    tables.extend([np.cos(twist).astype(np.float32), np.sin(twist).astype(np.float32)])
    return tables


def split(x):
    high = x.astype(bf16)
    return high, (x - high.astype(f32)).astype(bf16)


def mm(a, b):
    return jnp.dot(a, b, preferred_element_type=f32)


INPUTS = 17


def kernel(sky_ref, *refs):
    held, refs = refs[:INPUTS], refs[INPUTS:]
    out_ref, refs = refs[0], refs[1:]
    local_copies, refs = refs[:INPUTS], refs[INPUTS:]
    (
        sub_ref, cell_ref, ang_ref, seg_ref, waf_ref, mix_ref, knee_ref,
        f1h, f1l, f2h, f2l, f3h, f3l, f4h, f4l, tc_ref, ts_ref,
    ) = local_copies
    (
        in_sem,
        tab, lhs, iqu, local, cosw, sinw, wts, cs, xb, fs, wb,
        av, oh, acc, r1, s2, r2, r4, s3, r3,
        ag_recv, a1_recv, a2_recv, r1_recv, r2_recv, r4_recv, r3_recv,
        ag_send, a1_send, a2_send, r1_send, r2_send, r4_send, r3_send,
    ) = refs
    o = lax.axis_index("obs")
    j = lax.axis_index("dt")
    n_obs = lax.axis_size("obs")
    y, z = j >> 4, j & (NZ - 1)
    before, after = (o + n_obs - 1) & (n_obs - 1), (o + 1) & (n_obs - 1)

    offsets = sorted(
        ((dy, dz) for dy in range(-1, NY - 1) for dz in range(1 - NZ // 2, NZ // 2 + 1) if dy or dz),
        key=lambda p: abs(p[0]) + abs(p[1]))

    def chip(dy, dz):
        return ((y + dy) & (NY - 1)) * NZ + ((z + dz) & (NZ - 1))

    barrier = pltpu.get_barrier_semaphore()
    near = [chip(0, s) for s in range(-REACH, REACH + 1) if s] + [chip(s, 0) for s in range(1, NY)]
    for other in near:
        pl.semaphore_signal(barrier, inc=1, device_id={"dt": other}, device_id_type=MESH)
    for other in (before, after):
        pl.semaphore_signal(barrier, inc=1, device_id={"obs": other}, device_id_type=MESH)

    def load(k):
        return pltpu.make_async_copy(held[k], local_copies[k], in_sem.at[k])

    own_block = pltpu.make_async_copy(sky_ref, tab.at[j], in_sem.at[INPUTS])
    early, late = (2, 0, 3, 6), (1, 4, 5, *range(7, INPUTS))
    for k in (*early, *late):
        load(k).start()
    own_block.start()
    acc[...] = jnp.zeros_like(acc)
    for k in early:
        load(k).wait()

    double = 2.0 * ang_ref[0]
    cosw[...] = jnp.cos(double)
    sinw[...] = jnp.sin(double)
    local[...] = (sub_ref[0] - o * GROUP) & (n_obs * GROUP - 1)
    keep = jnp.where((seg_ref[...] & 1) == 0, 1.0, 0.0).astype(f32)
    rows = lax.broadcasted_iota(i32, (256, 128), 0)
    bins = (rows & 127) + 128 * lax.broadcasted_iota(i32, (256, 128), 1)
    freq = jnp.minimum(bins, NSAMP - bins).astype(f32)
    lanes = lax.broadcasted_iota(i32, (1, DET), 1)
    knee = knee_ref[...]
    knee_a = jnp.sum(jnp.where(lanes == 2 * j, knee, 0.0), axis=1, keepdims=True)
    knee_b = jnp.sum(jnp.where(lanes == 2 * j + 1, knee, 0.0), axis=1, keepdims=True)
    knees = jnp.where(rows < 128, knee_a, knee_b)
    square = freq * freq
    wts[...] = square / (square + knees * knees)

    pl.semaphore_wait(barrier, len(near) + 2)

    def sky_copy(src, slot, device):
        return pltpu.make_async_remote_copy(
            src_ref=src, dst_ref=tab.at[slot], send_sem=ag_send, recv_sem=ag_recv.at[slot],
            device_id=device, device_id_type=MESH)

    own = sky_ref

    def send(slot, device):
        sky_copy(tab.at[slot], slot, device).start()

    def to_before(slot):
        sky_copy(tab.at[slot], GROUP + slot, {"obs": before}).start()

    def arrive(slot):
        sky_copy(own, slot, {"obs": before}).wait_recv()

    for s in range(REACH, 0, -1):
        for step in (s, -s):
            sky_copy(own, j, {"dt": chip(0, step)}).start()
    for step in (2, 1, -1):
        sky_copy(own, j, {"dt": chip(step, 0)}).start()
    sky_copy(own, GROUP + j, {"obs": before}).start()
    sky_sends = 2 * REACH + NY

    def signs(s):
        return (1, -1) if 0 < s < NZ // 2 else (1,)

    def from_rows(s):
        for sign in signs(s):
            for dy in (1, -1, 2):
                slot = chip(dy, -sign * s)
                arrive(slot)
                to_before(slot)

    for s in range(1, NZ // 2 + 1):
        for sign in signs(s):
            slot = chip(0, -sign * s)
            arrive(slot)
            if s == REACH:
                for far in range(REACH if sign == 1 else REACH - 1, 0, -1):
                    send(slot, {"dt": chip(0, sign * far)})
                    sky_sends += 1
            for dy in (2, 1, -1):
                send(slot, {"dt": chip(dy, 0)})
            to_before(slot)
            sky_sends += NY
        if s >= LAG:
            from_rows(s - LAG)
    for s in range(NZ // 2 + 1 - LAG, NZ // 2 + 1):
        from_rows(s)
    sky_sends += NZ * (NY - 1)

    def prepare(first):
        for c in range(3):
            high, low = split(tab[first:first + GROUP, c, 0, :])
            row = c * WINDOW + first
            lhs[row:row + GROUP, :] = high
            lhs[3 * WINDOW + row:3 * WINDOW + row + GROUP, :] = low

    own_block.wait()
    prepare(0)

    arrive(GROUP + j)
    for step in offsets:
        arrive(GROUP + chip(*step))

    prepare(GROUP)
    for k in late:
        load(k).wait()

    def one_hot(row):
        return jnp.where(lax.broadcasted_iota(i32, (PIX, SPAN), 0) == row, 1.0, 0.0).astype(bf16)

    def gather(g, carry):
        base = pl.multiple_of(g * TILE, TILE)
        cells = cell_ref[0, pl.ds(base, TILE), :]
        subs = local[pl.ds(base, TILE), :]
        found = [[], [], []]
        for i in range(TILE):
            result = mm(lhs[...], one_hot(cells[i:i + 1]))
            mask = lax.broadcasted_iota(i32, (WINDOW, SPAN), 0) == subs[i:i + 1]
            for c in range(3):
                both = result[c * WINDOW:(c + 1) * WINDOW] + result[(3 + c) * WINDOW:(4 + c) * WINDOW]
                found[c].append(jnp.sum(jnp.where(mask, both, 0.0), axis=0, keepdims=True))
        for c in range(3):
            iqu[c, pl.ds(base, TILE), :] = jnp.concatenate(found[c], axis=0)
        return carry

    lax.fori_loop(0, DET // TILE, gather, 0)

    tod = keep * (iqu[0] + cosw[...] * iqu[1] + sinw[...] * iqu[2])
    wafer = jnp.broadcast_to(waf_ref[...], (DET, DET)).astype(f32)
    mixing = jnp.where(wafer.T == wafer, mix_ref[0].astype(f32), 0.0).astype(bf16)
    corr = tod + mm(mixing, tod.astype(bf16))
    for i in range(GROUP):
        cs[i] = corr[2 * i:2 * i + 2]

    def piece(src, dst, send_sem, recv_sem, here, there, device):
        return pltpu.make_async_remote_copy(
            src_ref=src.at[here], dst_ref=dst.at[there], send_sem=send_sem, recv_sem=recv_sem.at[there],
            device_id={"dt": device}, device_id_type=MESH)

    def spread(src, dst, send_sem, recv_sem, order):
        for step in order:
            other = chip(*step)
            piece(src, dst, send_sem, recv_sem, other, j, other).start()
        dst[pl.ds(j, 1)] = src[pl.ds(j, 1)]

    def take(src, dst, send_sem, recv_sem, source):
        piece(src, dst, send_sem, recv_sem, source, source, source).wait_recv()

    def all_left(src, send_sem, dst, recv_sem):
        def left(k, carry):
            piece(src, dst, send_sem, recv_sem, j, j, (j + 1) & (GROUP - 1)).wait_send()
            return carry

        lax.fori_loop(1, GROUP, left, 0)

    spread(cs, xb, a1_send, a1_recv, offsets[::-1])

    def sky_left(k, carry):
        sky_copy(own, j, {"obs": before}).wait_send()
        return carry

    lax.fori_loop(0, sky_sends, sky_left, 0)

    for step in offsets:
        take(cs, xb, a1_send, a1_recv, chip(*step))

    def exact_left(high, low, x):
        xh, xl = split(x)
        return mm(high[...], xh) + (mm(high[...], xl) + mm(low[...], xh))

    def exact_right(x, high, low):
        xh, xl = split(x)
        return mm(xh, high[...]) + (mm(xl, high[...]) + mm(xh, low[...]))

    pairs = jnp.concatenate([xb[i] for i in range(GROUP)], axis=0)
    series = jnp.concatenate([pairs[:, :128], pairs[:, 128:]], axis=0)
    part = exact_left(f1h, f1l, series)
    re, im = part[:256], part[256:]
    tc, ts = tc_ref[...], ts_ref[...]
    spec = exact_right(jnp.concatenate([re * tc + im * ts, im * tc - re * ts], axis=1), f2h, f2l)
    weight = wts[...]
    spec = spec * jnp.concatenate([weight, weight], axis=1)
    back = exact_right(spec, f3h, f3l)
    re, im = back[:, :128], back[:, 128:]
    turned = jnp.concatenate([re * tc - im * ts, re * ts + im * tc], axis=0)
    filtered = exact_left(f4h, f4l, turned)
    filtered = jnp.concatenate([filtered[:128], filtered[128:]], axis=1)
    for i in range(GROUP):
        fs[i] = filtered[2 * i:2 * i + 2]
    spread(fs, wb, a2_send, a2_recv, offsets)
    all_left(cs, a1_send, xb, a1_recv)

    def scatter(k, carry):
        dq = k >> 2
        g = ((y + k) & (NY - 1)) * 4 + (((z >> 2) + jnp.where(dq >= 2, 5 - dq, dq)) & 3)
        for i in range(TILE // 2):
            source = g * (TILE // 2) + i

            @pl.when(source != j)
            def _():
                take(fs, wb, a2_send, a2_recv, source)

        base = pl.multiple_of(g * TILE, TILE)
        cells = cell_ref[0, pl.ds(base, TILE), :]
        subs = local[pl.ds(base, TILE), :]
        weighted = jnp.concatenate([wb[g * (TILE // 2) + i] for i in range(TILE // 2)], axis=0) * keep
        value = [weighted, weighted * cosw[pl.ds(base, TILE), :], weighted * sinw[pl.ds(base, TILE), :]]
        for i in range(TILE):
            span = slice(i * SPAN, (i + 1) * SPAN)
            oh[:, span] = one_hot(cells[i:i + 1])
            mask = lax.broadcasted_iota(i32, (WINDOW, SPAN), 0) == subs[i:i + 1]
            for c in range(3):
                for t, x in enumerate(split(value[c][i:i + 1])):
                    k = 3 * t + c
                    av[k * WINDOW:(k + 1) * WINDOW, span] = jnp.where(mask, x.astype(f32), 0.0).astype(bf16)
        sums = lax.dot_general(av[...], oh[...], (((1,), (1,)), ((), ())), preferred_element_type=f32)
        for c in range(3):
            acc[c] += sums[c * WINDOW:(c + 1) * WINDOW] + sums[(3 + c) * WINDOW:(4 + c) * WINDOW]
        return carry

    lax.fori_loop(0, DET // TILE, scatter, 0)

    half = NZ // 2
    far_half = 1 - (z >> 3)
    halves = (far_half, 1 - far_half)

    def block(row, part):
        return acc.at[:, pl.ds(pl.multiple_of(row * NZ + part * half, half), half), :]

    def to_next(row, part):
        return pltpu.make_async_remote_copy(
            src_ref=block(NY + row, part), dst_ref=r1.at[part, row], send_sem=r1_send,
            recv_sem=r1_recv.at[part, row], device_id={"obs": after}, device_id_type=MESH)

    def to_row(row, part, slot):
        return pltpu.make_async_remote_copy(
            src_ref=s2.at[part, row], dst_ref=r2.at[part, slot], send_sem=r2_send,
            recv_sem=r2_recv.at[part, slot], device_id={"dt": row * NZ + z}, device_id_type=MESH)

    def by_neighbour(part, side):
        step = 1 - 2 * side
        row = (y + step) & (NY - 1)
        return pltpu.make_async_remote_copy(
            src_ref=s2.at[part, (y + 2) & (NY - 1), :, :, pl.ds(side * (PIX // 2), PIX // 2)],
            dst_ref=r4.at[part, side], send_sem=r4_send, recv_sem=r4_recv.at[part, side],
            device_id={"dt": row * NZ + z}, device_id_type=MESH)

    def to_owner(other, slot):
        return pltpu.make_async_remote_copy(
            src_ref=s3.at[other], dst_ref=r3.at[slot], send_sem=r3_send, recv_sem=r3_recv.at[slot],
            device_id={"dt": y * NZ + other}, device_id_type=MESH)

    turns = [(y + k) & (NY - 1) for k in (2, 1, 3, 0)]
    for part in halves:
        for row in turns:
            to_next(row, part).start()
    for part in halves:
        for k, row in enumerate(turns):
            to_next(row, part).wait_recv()
            s2[part, row] = block(row, part)[...] + r1[part, row]
            if k == 0:
                for side in range(2):
                    by_neighbour(part, side).start()
        for side in range(2):
            row = (y + 1 - 2 * side) & (NY - 1)
            lanes = slice(side * (PIX // 2), (side + 1) * (PIX // 2))
            by_neighbour(part, side).wait_recv()
            s2[part, row, :, :, lanes] = s2[part, row, :, :, lanes] + r4[part, side]
            to_row(row, part, y).start()
    for part in halves:
        total = s2[part, y]
        for row in turns[1:NY - 1]:
            to_row(row, part, row).wait_recv()
            total = total + r2[part, row]
        for k in range(half):
            other = part * half + k
            s3[other] = total[:, k, :]

            @pl.when(other != z)
            def _():
                to_owner(other, z).start()

    r3[pl.ds(z, 1)] = s3[pl.ds(z, 1)]
    for k in range(1, NZ):
        other = (z + k) & (NZ - 1)
        to_owner(other, other).wait_recv()
    result = r3[0]
    for k in range(1, NZ):
        result = result + r3[k]
    out_ref[...] = result[:, None, :]

    all_left(fs, a2_send, wb, a2_recv)
    for part in range(2):
        for row in range(NY):
            to_next(row, part).wait_send()
        for side in range(2):
            by_neighbour(part, side).wait_send()
            to_row((y + 1 - 2 * side) & (NY - 1), part, y).wait_send()
    for k in range(1, NZ):
        to_owner((z + k) & (NZ - 1), z).wait_send()


def body(sky_map, submap_of, pixel_cell, angles, intervals, wafer_of, mixing, knee):
    vmem = pl.BlockSpec(memory_space=pltpu.VMEM)
    tables = [jnp.asarray(t) for t in dft_tables()]
    args = [jnp.transpose(sky_map, (1, 0, 2)), submap_of, pixel_cell, angles, intervals, wafer_of, mixing, knee, *tables]
    dma = pltpu.SemaphoreType.DMA
    result = pl.pallas_call(
        kernel,
        out_shape=jax.ShapeDtypeStruct((3, 1, PIX), f32),
        in_specs=[pl.BlockSpec(memory_space=pl.ANY)] * len(args),
        out_specs=vmem,
        scratch_shapes=[
            *[pltpu.VMEM(a.shape, a.dtype) for a in args[1:]],
            dma((INPUTS + 1,)),
            pltpu.VMEM((WINDOW, 3, 1, PIX), f32),
            pltpu.VMEM((6 * WINDOW, PIX), bf16),
            pltpu.VMEM((3, DET, SPAN), f32),
            pltpu.VMEM((DET, SPAN), i32),
            pltpu.VMEM((DET, SPAN), f32),
            pltpu.VMEM((DET, SPAN), f32),
            pltpu.VMEM((256, 128), f32),
            pltpu.VMEM((GROUP, 2, SPAN), f32),
            pltpu.VMEM((GROUP, 2, SPAN), f32),
            pltpu.VMEM((GROUP, 2, SPAN), f32),
            pltpu.VMEM((GROUP, 2, SPAN), f32),
            pltpu.VMEM((6 * WINDOW, TILE * SPAN), bf16),
            pltpu.VMEM((PIX, TILE * SPAN), bf16),
            pltpu.VMEM((3, WINDOW, PIX), f32),
            pltpu.VMEM((2, NY, 3, NZ // 2, PIX), f32),
            pltpu.VMEM((2, NY, 3, NZ // 2, PIX), f32),
            pltpu.VMEM((2, NY, 3, NZ // 2, PIX), f32),
            pltpu.VMEM((2, 2, 3, NZ // 2, PIX // 2), f32),
            pltpu.VMEM((NZ, 3, PIX), f32),
            pltpu.VMEM((NZ, 3, PIX), f32),
            dma((WINDOW,)), dma((GROUP,)), dma((GROUP,)), dma((2, NY)), dma((2, NY)), dma((2, 2)), dma((NZ,)),
            dma, dma, dma, dma, dma, dma, dma,
        ],
        compiler_params=pltpu.CompilerParams(
            collective_id=0, has_side_effects=True, vmem_limit_bytes=60 << 20),
        name="mapmaker",
    )(*args)
    return jnp.transpose(result, (1, 0, 2))


def solution(mesh):
    return jax.shard_map(
        body,
        mesh=mesh,
        in_specs=(
            P(("obs", "dt"), None, None),
            P("obs", None, "dt"),
            P("obs", None, "dt"),
            P("obs", None, "dt"),
            P("obs", "dt"),
            P("obs", None),
            P("obs", None, None),
            P("obs", None),
        ),
        out_specs=P(("obs", "dt"), None, None),
        check_vma=False,
    )
```

```python
import math

import jax
import jax.numpy as jnp
import ml_dtypes
import numpy as np
from jax import lax
from jax.experimental import pallas as pl
from jax.experimental.pallas import tpu as pltpu
from jax.sharding import PartitionSpec as P

MESH = pl.DeviceIdType.MESH
f32, bf16, i32 = jnp.float32, jnp.bfloat16, jnp.int32

DET = 128
SPAN = 256
PIX = 512
GROUP = 64
NY, NZ = 4, 16
REACH = 4
LAG = 3
WINDOW = 2 * GROUP
NSAMP = GROUP * SPAN
TILE = 8


def split_np(x):
    high = x.astype(ml_dtypes.bfloat16)
    low = (x - high.astype(np.float64)).astype(ml_dtypes.bfloat16)
    return high, low


def dft_tables():
    n = 128
    row = np.arange(256)
    row_det, row_n1 = row % 2, 2 * ((row % n) // 2) + row // n
    col_det, col_k1 = row // n, row % n
    same = (row_det[:, None] == col_det[None, :]).astype(np.float64)
    turn = 2.0 * np.pi * ((row_n1[:, None] * col_k1[None, :]) % n) / n
    cos_part, sin_part = same * np.cos(turn), -same * np.sin(turn)
    last = np.concatenate([cos_part, sin_part], axis=1)
    first = np.ascontiguousarray(last.T)
    index = np.arange(n)
    angle = 2.0 * np.pi * ((index[:, None] * index[None, :]) % n) / n
    c, s = np.cos(angle), np.sin(angle)
    forward = np.block([[c, -s], [s, c]])
    backward = np.block([[c, s], [-s, c]]) / NSAMP
    twist = 2.0 * np.pi * (col_k1[:, None] * index[None, :]) / NSAMP
    tables = []
    for x in (first, forward, backward, last):
        tables.extend(split_np(x))
    tables.extend([np.cos(twist).astype(np.float32), np.sin(twist).astype(np.float32)])
    return tables


def split(x):
    high = x.astype(bf16)
    return high, (x - high.astype(f32)).astype(bf16)


def mm(a, b):
    return jnp.dot(a, b, preferred_element_type=f32)


INPUTS = 17


def kernel(sky_ref, *refs):
    held, refs = refs[:INPUTS], refs[INPUTS:]
    out_ref, refs = refs[0], refs[1:]
    local_copies, refs = refs[:INPUTS], refs[INPUTS:]
    (
        sub_ref, cell_ref, ang_ref, seg_ref, waf_ref, mix_ref, knee_ref,
        f1h, f1l, f2h, f2l, f3h, f3l, f4h, f4l, tc_ref, ts_ref,
    ) = local_copies
    (
        in_sem,
        tab, lhs, iqu, local, cosw, sinw, wts, cs, xb, fs, wb,
        av, oh, acc, r1, s2, r2, r4, s3, r3,
        ag_recv, a1_recv, a2_recv, r1_recv, r2_recv, r4_recv, r3_recv,
        ag_send, a1_send, a2_send, r1_send, r2_send, r4_send, r3_send,
    ) = refs
    o = lax.axis_index("obs")
    j = lax.axis_index("dt")
    n_obs = lax.axis_size("obs")
    y, z = j >> 4, j & (NZ - 1)
    before, after = (o + n_obs - 1) & (n_obs - 1), (o + 1) & (n_obs - 1)

    offsets = sorted(
        ((dy, dz) for dy in range(-1, NY - 1) for dz in range(1 - NZ // 2, NZ // 2 + 1) if dy or dz),
        key=lambda p: abs(p[0]) + abs(p[1]))

    def chip(dy, dz):
        return ((y + dy) & (NY - 1)) * NZ + ((z + dz) & (NZ - 1))

    barrier = pltpu.get_barrier_semaphore()
    near = [chip(0, s) for s in range(-REACH, REACH + 1) if s] + [chip(s, 0) for s in range(1, NY)]
    for other in near:
        pl.semaphore_signal(barrier, inc=1, device_id={"dt": other}, device_id_type=MESH)
    for other in (before, after):
        pl.semaphore_signal(barrier, inc=1, device_id={"obs": other}, device_id_type=MESH)

    def load(k):
        return pltpu.make_async_copy(held[k], local_copies[k], in_sem.at[k])

    own_block = pltpu.make_async_copy(sky_ref, tab.at[j], in_sem.at[INPUTS])
    early, late = (2, 0, 3, 6), (1, 4, 5, *range(7, INPUTS))
    for k in (*early, *late):
        load(k).start()
    own_block.start()
    acc[...] = jnp.zeros_like(acc)
    for k in early:
        load(k).wait()

    double = 2.0 * ang_ref[0]
    cosw[...] = jnp.cos(double)
    sinw[...] = jnp.sin(double)
    local[...] = (sub_ref[0] - o * GROUP) & (n_obs * GROUP - 1)
    keep = jnp.where((seg_ref[...] & 1) == 0, 1.0, 0.0).astype(f32)
    rows = lax.broadcasted_iota(i32, (256, 128), 0)
    bins = (rows & 127) + 128 * lax.broadcasted_iota(i32, (256, 128), 1)
    freq = jnp.minimum(bins, NSAMP - bins).astype(f32)
    lanes = lax.broadcasted_iota(i32, (1, DET), 1)
    knee = knee_ref[...]
    knee_a = jnp.sum(jnp.where(lanes == 2 * j, knee, 0.0), axis=1, keepdims=True)
    knee_b = jnp.sum(jnp.where(lanes == 2 * j + 1, knee, 0.0), axis=1, keepdims=True)
    knees = jnp.where(rows < 128, knee_a, knee_b)
    square = freq * freq
    wts[...] = square / (square + knees * knees)

    pl.semaphore_wait(barrier, len(near) + 2)

    def sky_copy(src, slot, device):
        return pltpu.make_async_remote_copy(
            src_ref=src, dst_ref=tab.at[slot], send_sem=ag_send, recv_sem=ag_recv.at[slot],
            device_id=device, device_id_type=MESH)

    own = sky_ref

    def send(slot, device):
        sky_copy(tab.at[slot], slot, device).start()

    def to_before(slot):
        sky_copy(tab.at[slot], GROUP + slot, {"obs": before}).start()

    def arrive(slot):
        sky_copy(own, slot, {"obs": before}).wait_recv()

    for s in range(REACH, 0, -1):
        for step in (s, -s):
            sky_copy(own, j, {"dt": chip(0, step)}).start()
    for step in (2, 1, -1):
        sky_copy(own, j, {"dt": chip(step, 0)}).start()
    sky_copy(own, GROUP + j, {"obs": before}).start()
    sky_sends = 2 * REACH + NY

    def signs(s):
        return (1, -1) if 0 < s < NZ // 2 else (1,)

    def from_rows(s):
        for sign in signs(s):
            for dy in (1, -1, 2):
                slot = chip(dy, -sign * s)
                arrive(slot)
                to_before(slot)

    for s in range(1, NZ // 2 + 1):
        for sign in signs(s):
            slot = chip(0, -sign * s)
            arrive(slot)
            if s == REACH:
                for far in range(REACH if sign == 1 else REACH - 1, 0, -1):
                    send(slot, {"dt": chip(0, sign * far)})
                    sky_sends += 1
            for dy in (2, 1, -1):
                send(slot, {"dt": chip(dy, 0)})
            to_before(slot)
            sky_sends += NY
        if s >= LAG:
            from_rows(s - LAG)
    for s in range(NZ // 2 + 1 - LAG, NZ // 2 + 1):
        from_rows(s)
    sky_sends += NZ * (NY - 1)

    def prepare(first):
        for c in range(3):
            high, low = split(tab[first:first + GROUP, c, 0, :])
            row = c * WINDOW + first
            lhs[row:row + GROUP, :] = high
            lhs[3 * WINDOW + row:3 * WINDOW + row + GROUP, :] = low

    own_block.wait()
    prepare(0)

    for dy in (0, 1, -1, 2):
        for dz in sorted(range(1 - NZ // 2, NZ // 2 + 1), key=abs):
            arrive(GROUP + chip(dy, dz))
        first = pl.multiple_of(GROUP + ((y + dy) & (NY - 1)) * NZ, NZ)
        for c in range(3):
            high, low = split(tab[pl.ds(first, NZ), c, 0, :])
            lhs[pl.ds(c * WINDOW + first, NZ), :] = high
            lhs[pl.ds((3 + c) * WINDOW + first, NZ), :] = low
    for k in late:
        load(k).wait()

    def one_hot(row):
        return jnp.where(lax.broadcasted_iota(i32, (PIX, SPAN), 0) == row, 1.0, 0.0).astype(bf16)

    def gather(g, carry):
        base = pl.multiple_of(g * TILE, TILE)
        cells = cell_ref[0, pl.ds(base, TILE), :]
        subs = local[pl.ds(base, TILE), :]
        found = [[], [], []]
        for i in range(TILE):
            result = mm(lhs[...], one_hot(cells[i:i + 1]))
            mask = lax.broadcasted_iota(i32, (WINDOW, SPAN), 0) == subs[i:i + 1]
            for c in range(3):
                both = result[c * WINDOW:(c + 1) * WINDOW] + result[(3 + c) * WINDOW:(4 + c) * WINDOW]
                found[c].append(jnp.sum(jnp.where(mask, both, 0.0), axis=0, keepdims=True))
        for c in range(3):
            iqu[c, pl.ds(base, TILE), :] = jnp.concatenate(found[c], axis=0)
        return carry

    lax.fori_loop(0, DET // TILE, gather, 0)

    tod = keep * (iqu[0] + cosw[...] * iqu[1] + sinw[...] * iqu[2])
    wafer = jnp.broadcast_to(waf_ref[...], (DET, DET)).astype(f32)
    mixing = jnp.where(wafer.T == wafer, mix_ref[0].astype(f32), 0.0).astype(bf16)
    corr = tod + mm(mixing, tod.astype(bf16))
    for i in range(GROUP):
        cs[i] = corr[2 * i:2 * i + 2]

    def piece(src, dst, send_sem, recv_sem, here, there, device):
        return pltpu.make_async_remote_copy(
            src_ref=src.at[here], dst_ref=dst.at[there], send_sem=send_sem, recv_sem=recv_sem.at[there],
            device_id={"dt": device}, device_id_type=MESH)

    def spread(src, dst, send_sem, recv_sem, order):
        for step in order:
            other = chip(*step)
            piece(src, dst, send_sem, recv_sem, other, j, other).start()
        dst[pl.ds(j, 1)] = src[pl.ds(j, 1)]

    def take(src, dst, send_sem, recv_sem, source):
        piece(src, dst, send_sem, recv_sem, source, source, source).wait_recv()

    def all_left(src, send_sem, dst, recv_sem):
        def left(k, carry):
            piece(src, dst, send_sem, recv_sem, j, j, (j + 1) & (GROUP - 1)).wait_send()
            return carry

        lax.fori_loop(1, GROUP, left, 0)

    spread(cs, xb, a1_send, a1_recv, offsets[::-1])

    def sky_left(k, carry):
        sky_copy(own, j, {"obs": before}).wait_send()
        return carry

    lax.fori_loop(0, sky_sends, sky_left, 0)

    for step in offsets:
        take(cs, xb, a1_send, a1_recv, chip(*step))

    def exact_left(high, low, x):
        xh, xl = split(x)
        return mm(high[...], xh) + (mm(high[...], xl) + mm(low[...], xh))

    def exact_right(x, high, low):
        xh, xl = split(x)
        return mm(xh, high[...]) + (mm(xl, high[...]) + mm(xh, low[...]))

    pairs = jnp.concatenate([xb[i] for i in range(GROUP)], axis=0)
    series = jnp.concatenate([pairs[:, :128], pairs[:, 128:]], axis=0)
    part = exact_left(f1h, f1l, series)
    re, im = part[:256], part[256:]
    tc, ts = tc_ref[...], ts_ref[...]
    spec = exact_right(jnp.concatenate([re * tc + im * ts, im * tc - re * ts], axis=1), f2h, f2l)
    weight = wts[...]
    spec = spec * jnp.concatenate([weight, weight], axis=1)
    back = exact_right(spec, f3h, f3l)
    re, im = back[:, :128], back[:, 128:]
    turned = jnp.concatenate([re * tc - im * ts, re * ts + im * tc], axis=0)
    filtered = exact_left(f4h, f4l, turned)
    filtered = jnp.concatenate([filtered[:128], filtered[128:]], axis=1)
    for i in range(GROUP):
        fs[i] = filtered[2 * i:2 * i + 2]
    spread(fs, wb, a2_send, a2_recv, offsets)
    all_left(cs, a1_send, xb, a1_recv)

    def scatter(k, carry):
        dq = k >> 2
        g = ((y + k) & (NY - 1)) * 4 + (((z >> 2) + jnp.where(dq >= 2, 5 - dq, dq)) & 3)
        for i in range(TILE // 2):
            source = g * (TILE // 2) + i

            @pl.when(source != j)
            def _():
                take(fs, wb, a2_send, a2_recv, source)

        base = pl.multiple_of(g * TILE, TILE)
        cells = cell_ref[0, pl.ds(base, TILE), :]
        subs = local[pl.ds(base, TILE), :]
        weighted = jnp.concatenate([wb[g * (TILE // 2) + i] for i in range(TILE // 2)], axis=0) * keep
        value = [weighted, weighted * cosw[pl.ds(base, TILE), :], weighted * sinw[pl.ds(base, TILE), :]]
        for i in range(TILE):
            span = slice(i * SPAN, (i + 1) * SPAN)
            oh[:, span] = one_hot(cells[i:i + 1])
            mask = lax.broadcasted_iota(i32, (WINDOW, SPAN), 0) == subs[i:i + 1]
            for c in range(3):
                for t, x in enumerate(split(value[c][i:i + 1])):
                    k = 3 * t + c
                    av[k * WINDOW:(k + 1) * WINDOW, span] = jnp.where(mask, x.astype(f32), 0.0).astype(bf16)
        sums = lax.dot_general(av[...], oh[...], (((1,), (1,)), ((), ())), preferred_element_type=f32)
        for c in range(3):
            acc[c] += sums[c * WINDOW:(c + 1) * WINDOW] + sums[(3 + c) * WINDOW:(4 + c) * WINDOW]
        return carry

    lax.fori_loop(0, DET // TILE, scatter, 0)

    half = NZ // 2
    far_half = 1 - (z >> 3)
    halves = (far_half, 1 - far_half)

    def block(row, part):
        return acc.at[:, pl.ds(pl.multiple_of(row * NZ + part * half, half), half), :]

    def to_next(row, part):
        return pltpu.make_async_remote_copy(
            src_ref=block(NY + row, part), dst_ref=r1.at[part, row], send_sem=r1_send,
            recv_sem=r1_recv.at[part, row], device_id={"obs": after}, device_id_type=MESH)

    def to_row(row, part, slot):
        return pltpu.make_async_remote_copy(
            src_ref=s2.at[part, row], dst_ref=r2.at[part, slot], send_sem=r2_send,
            recv_sem=r2_recv.at[part, slot], device_id={"dt": row * NZ + z}, device_id_type=MESH)

    def by_neighbour(part, side):
        step = 1 - 2 * side
        row = (y + step) & (NY - 1)
        return pltpu.make_async_remote_copy(
            src_ref=s2.at[part, (y + 2) & (NY - 1), :, :, pl.ds(side * (PIX // 2), PIX // 2)],
            dst_ref=r4.at[part, side], send_sem=r4_send, recv_sem=r4_recv.at[part, side],
            device_id={"dt": row * NZ + z}, device_id_type=MESH)

    def to_owner(other, slot):
        return pltpu.make_async_remote_copy(
            src_ref=s3.at[other], dst_ref=r3.at[slot], send_sem=r3_send, recv_sem=r3_recv.at[slot],
            device_id={"dt": y * NZ + other}, device_id_type=MESH)

    turns = [(y + k) & (NY - 1) for k in (2, 1, 3, 0)]
    for part in halves:
        for row in turns:
            to_next(row, part).start()
    for part in halves:
        for k, row in enumerate(turns):
            to_next(row, part).wait_recv()
            s2[part, row] = block(row, part)[...] + r1[part, row]
            if k == 0:
                for side in range(2):
                    by_neighbour(part, side).start()
        for side in range(2):
            row = (y + 1 - 2 * side) & (NY - 1)
            lanes = slice(side * (PIX // 2), (side + 1) * (PIX // 2))
            by_neighbour(part, side).wait_recv()
            s2[part, row, :, :, lanes] = s2[part, row, :, :, lanes] + r4[part, side]
            to_row(row, part, y).start()
    for part in halves:
        total = s2[part, y]
        for row in turns[1:NY - 1]:
            to_row(row, part, row).wait_recv()
            total = total + r2[part, row]
        for k in range(half):
            other = part * half + k
            s3[other] = total[:, k, :]

            @pl.when(other != z)
            def _():
                to_owner(other, z).start()

    r3[pl.ds(z, 1)] = s3[pl.ds(z, 1)]
    for k in range(1, NZ):
        other = (z + k) & (NZ - 1)
        to_owner(other, other).wait_recv()
    result = r3[0]
    for k in range(1, NZ):
        result = result + r3[k]
    out_ref[...] = result[:, None, :]

    all_left(fs, a2_send, wb, a2_recv)
    for part in range(2):
        for row in range(NY):
            to_next(row, part).wait_send()
        for side in range(2):
            by_neighbour(part, side).wait_send()
            to_row((y + 1 - 2 * side) & (NY - 1), part, y).wait_send()
    for k in range(1, NZ):
        to_owner((z + k) & (NZ - 1), z).wait_send()


def body(sky_map, submap_of, pixel_cell, angles, intervals, wafer_of, mixing, knee):
    vmem = pl.BlockSpec(memory_space=pltpu.VMEM)
    tables = [jnp.asarray(t) for t in dft_tables()]
    args = [jnp.transpose(sky_map, (1, 0, 2)), submap_of, pixel_cell, angles, intervals, wafer_of, mixing, knee, *tables]
    dma = pltpu.SemaphoreType.DMA
    result = pl.pallas_call(
        kernel,
        out_shape=jax.ShapeDtypeStruct((3, 1, PIX), f32),
        in_specs=[pl.BlockSpec(memory_space=pl.ANY)] * len(args),
        out_specs=vmem,
        scratch_shapes=[
            *[pltpu.VMEM(a.shape, a.dtype) for a in args[1:]],
            dma((INPUTS + 1,)),
            pltpu.VMEM((WINDOW, 3, 1, PIX), f32),
            pltpu.VMEM((6 * WINDOW, PIX), bf16),
            pltpu.VMEM((3, DET, SPAN), f32),
            pltpu.VMEM((DET, SPAN), i32),
            pltpu.VMEM((DET, SPAN), f32),
            pltpu.VMEM((DET, SPAN), f32),
            pltpu.VMEM((256, 128), f32),
            pltpu.VMEM((GROUP, 2, SPAN), f32),
            pltpu.VMEM((GROUP, 2, SPAN), f32),
            pltpu.VMEM((GROUP, 2, SPAN), f32),
            pltpu.VMEM((GROUP, 2, SPAN), f32),
            pltpu.VMEM((6 * WINDOW, TILE * SPAN), bf16),
            pltpu.VMEM((PIX, TILE * SPAN), bf16),
            pltpu.VMEM((3, WINDOW, PIX), f32),
            pltpu.VMEM((2, NY, 3, NZ // 2, PIX), f32),
            pltpu.VMEM((2, NY, 3, NZ // 2, PIX), f32),
            pltpu.VMEM((2, NY, 3, NZ // 2, PIX), f32),
            pltpu.VMEM((2, 2, 3, NZ // 2, PIX // 2), f32),
            pltpu.VMEM((NZ, 3, PIX), f32),
            pltpu.VMEM((NZ, 3, PIX), f32),
            dma((WINDOW,)), dma((GROUP,)), dma((GROUP,)), dma((2, NY)), dma((2, NY)), dma((2, 2)), dma((NZ,)),
            dma, dma, dma, dma, dma, dma, dma,
        ],
        compiler_params=pltpu.CompilerParams(
            collective_id=0, has_side_effects=True, vmem_limit_bytes=60 << 20),
        name="mapmaker",
    )(*args)
    return jnp.transpose(result, (1, 0, 2))


def solution(mesh):
    return jax.shard_map(
        body,
        mesh=mesh,
        in_specs=(
            P(("obs", "dt"), None, None),
            P("obs", None, "dt"),
            P("obs", None, "dt"),
            P("obs", None, "dt"),
            P("obs", "dt"),
            P("obs", None),
            P("obs", None, None),
            P("obs", None),
        ),
        out_specs=P(("obs", "dt"), None, None),
        check_vma=False,
    )
```
